128 devices in a mesh: face: 8 (over y, x_hi), lon: 16 (over z, x_lo, core).
Axes of the slice: x: 4 (x_hi: 2, x_lo: 2; x = x_hi * 2 + x_lo), y: 4, z: 4, core: 2. Of those that a mesh axis runs over, the one named last changes fastest.
Arguments:
- source: bfloat16 [4096, 8, 128], P(('face', 'lon')), may hold values from -6 to 6
- intersection_weight: bfloat16 [4096, 4, 128, 128], P(('face', 'lon')), may hold values from -0.5 to 0.5
- dest_tile: int32 [4096, 4], P(('face', 'lon')), may hold values from 0 to 127, all different within a row; in each aligned block of 32 rows (0 to 31, 32 to 63, ...) at most 2 rows name the same one
- dest_row: int32 [4096, 4], P(('face', 'lon')), may hold values from 0 to 63
- prior_state: bfloat16 [8, 256, 4096], P(None, 'face', 'lon'), may hold values from -6 to 6
- lift_weight: bfloat16 [8, 64], replicated, may hold values from -9 to 9
- kernel: bfloat16 [9, 64, 64], replicated, may hold values from -0.23570226 to 0.23570226
- readout_weights: bfloat16 [64, 8], replicated, may hold values from -0.75 to 0.75
Outputs:
- remapped_reference: bfloat16 [8, 256, 4096], P(None, 'face', 'lon')
- network_estimate: bfloat16 [8, 256, 4096], P(None, 'face', 'lon')
- grad_lift: float32 [8, 64], replicated
- grad_kernel: float32 [9, 64, 64], replicated
- grad_head: float32 [64, 8], replicated
The draws below stay inside these ranges and needn't reach their ends.
Inputs may be any that keep to these rules, and one draw needn't show every extreme that they name: `dest_tile`: the 4 intersections of a source block name distinct devices; the source blocks of one device name one device at most 2 times, and exactly 2 times for some device.
All inputs are finite; a program needn't handle non-finite values.
Results may differ from the reference program's by a relative error of at most 0.0013.
The reference program's roundings to bfloat16 on the way count: a program that leaves them out, or rounds other values in their place, can miss the bound.
Values may be sent and summed in bfloat16 or wider, within the bound.
A program may use at most 128 MiB of HBM per device.

```python
import math
import jax
import jax.numpy as jnp
import numpy as np
from jax import lax

QUANTITY_TOTAL = 8
WIDTH = 64
BLOCK = 128
K = 4
TAPS = 9
S_DEV = 32
ZONE_PARALLELS = 32
W_DEV = 256
TB = 64
CAP = 2
SRC = 4096
NLAT = 256
MERIDIAN_TOTAL = 4096
N_FACE = 8
N_LON = 16
DEVICES = 128


def draw_lift_weight(key, part):
    first_key = jax.random.fold_in(key, 11)
    second_key = jax.random.fold_in(key, 12)
    spread = QUANTITY_TOTAL ** (-0.5)
    private = jnp.clip(jax.random.normal(first_key, (QUANTITY_TOTAL, WIDTH), jnp.float32) * spread, -4.0 * spread, 4.0 * spread)
    shared = jax.random.uniform(second_key, (QUANTITY_TOTAL, 1), jnp.float32, 4.0, 7.0)
    signs = jnp.where(jnp.arange(QUANTITY_TOTAL) % 2 == 0, 1.0, -1.0).astype(jnp.float32)[:, None]
    return (private + shared * signs).astype(jnp.bfloat16)


def draw_kernel(key, part):
    base_key = jax.random.fold_in(key, 21)
    spread = (2.0 * TAPS * WIDTH) ** (-0.5)
    base = jnp.clip(jax.random.normal(base_key, (TAPS, WIDTH, WIDTH), jnp.float32) * spread, -4.0 * spread, 4.0 * spread)
    return (base - jnp.roll(base, 1, axis=1)).astype(jnp.bfloat16)


def with_ends(result, key, low, high):
    shape = result.shape
    spot = [jax.random.randint(jax.random.fold_in(key, axis), (), 0, shape[axis]) for axis in range(len(shape))]
    result = result.at[tuple(spot)].set(low)
    longest = shape.index(max(shape))
    spot[longest] = (spot[longest] + 1) % shape[longest]
    return result.at[tuple(spot)].set(high)


def levels(stream_key, shape, shards, smallest, largest):
    factor_of = 1.0
    for axis_at, blocks in shards:
        steps = jax.random.uniform(jax.random.fold_in(jax.random.fold_in(stream_key, 6), axis_at), (blocks,), jnp.float32, smallest / len(shards), largest / len(shards))
        factor_of = factor_of * jnp.repeat(jnp.exp(steps), shape[axis_at] // blocks).reshape((-1,) + (1,) * (len(shape) - 1 - axis_at))
    return factor_of


def routed_block(rng, own, number, rows, count, top, bound, skew):
    ranking = jax.random.permutation(rng, count)
    packed, usual = portions_of(count, rows * top, bound, skew, True), portions_of(count, rows * top, bound, skew, False)
    places = jnp.arange(count)

    def named(lengths, rotation):
        used = int((lengths > 0).sum())
        fixed = max(1, used // 4)
        shifted = fixed + (places - fixed + rotation * (used - fixed)) % max(1, count - fixed)
        return jnp.zeros((count,), jnp.int32).at[ranking[jnp.where(places < fixed, places, shifted)]].set(jnp.asarray(lengths, jnp.int32))

    lengths = jnp.where(number % 4 == 0, named(packed, number // 4), named(usual, number - number // 4 - 1))
    mixed = jax.random.permutation(jax.random.fold_in(own, 3), count)
    giver, receiver = mixed[0:count // 2 * 2:2], mixed[1:count // 2 * 2:2]
    room = jnp.minimum(lengths[giver] - 1, bound - lengths[receiver]) // 2
    room = jnp.where((giver == ranking[0]) | (receiver == ranking[0]) | (lengths[receiver] == 0), 0, jnp.maximum(room, 0))
    shifted = jax.random.randint(jax.random.fold_in(own, 4), (count // 2,), 0, 1 << 20) % (room + 1)
    lengths = lengths.at[giver].add(-shifted).at[receiver].add(shifted)
    items = jnp.searchsorted(jnp.cumsum(lengths), jnp.arange(rows * top), side="right").astype(jnp.int32)
    listing = items.reshape(top, rows).T
    listing = listing[jax.random.permutation(jax.random.fold_in(own, 1), rows)]
    rotation = jax.random.randint(jax.random.fold_in(own, 2), (rows, 1), 0, top)
    return jnp.take_along_axis(listing, (jnp.arange(top)[None, :] + rotation) % top, axis=1)


def portions_of(amount, total, reach, skew, full):
    weights = [(1 << 20) // math.isqrt(rank ** skew) + 1 for rank in range(1, amount + 1)]
    largest = reach if full else min(reach, max(-(-total // amount), total * weights[0] // sum(weights)))
    least = 1 if total - largest >= amount - 1 else 0
    given, rest = [largest] + [least] * (amount - 1), total - largest - least * (amount - 1)
    while rest > 0:
        candidates = [i for i in range(1, amount) if given[i] < largest] or [i for i in range(1, amount) if given[i] < reach]
        whole, budget = sum([weights[i] for i in candidates]), rest
        for i in candidates:
            more = min(reach - given[i], max(1, budget * weights[i] // whole), rest)
            given[i] = given[i] + more
            rest = rest - more
    return np.array(given)


def normal_values(own_key, dims, scale, limit, split=(), held_as=jnp.bfloat16):
    result = scale * jax.random.normal(own_key, dims, jnp.float32)
    if split:
        result = result * levels(own_key, dims, split, -0.22, 0.18)
    return jnp.clip(result, -limit, limit).astype(held_as)


def setup_inputs(seed: int = 0) -> dict:
    streams_of = jax.random.split(jax.random.key(seed), 9)
    source = normal_values(streams_of[0], (SRC, QUANTITY_TOTAL, BLOCK), 1.0, 6.0, ((0, 128),))
    intersection_weight = normal_values(streams_of[1], (SRC, K, BLOCK, BLOCK), BLOCK ** -0.5, 0.5, ((0, 128),))
    dest_tile_keys = jax.random.split(jax.random.fold_in(streams_of[2], 1), SRC // S_DEV)
    dest_tile_turns = jax.random.permutation(jax.random.fold_in(streams_of[2], 3), SRC // S_DEV)
    dest_tile = jax.vmap(lambda own, number: routed_block(jax.random.fold_in(streams_of[2], 2), own, number, S_DEV, DEVICES, K, CAP, 2))(dest_tile_keys, dest_tile_turns).reshape((SRC, K))
    dest_row = with_ends(jax.random.randint(streams_of[3], (SRC, K), 0, TB), jax.random.fold_in(streams_of[3], 1), 0, TB - 1).astype(jnp.int32)
    prior_state = normal_values(streams_of[4], (QUANTITY_TOTAL, NLAT, MERIDIAN_TOTAL), 1.0, 6.0, ((1, 8), (2, 16)))
    lift_weight = draw_lift_weight(jax.random.fold_in(streams_of[8], 71), 0)
    kernel = draw_kernel(jax.random.fold_in(streams_of[8], 71), 0)
    readout_weights = normal_values(streams_of[7], (WIDTH, QUANTITY_TOTAL), WIDTH ** -0.5, 0.75)
    return {"source": source, "intersection_weight": intersection_weight, "dest_tile": dest_tile, "dest_row": dest_row, "prior_state": prior_state, "lift_weight": lift_weight, "kernel": kernel, "readout_weights": readout_weights}


def wrap_lon(field):
    return jnp.concatenate([field[:, :, -1:], field, field[:, :, :1]], 2)

def conv_taps(kernel, padded, out_rows, out_cols):
    running = jnp.zeros((kernel.shape[2], out_rows * out_cols), jnp.float32)
    for tap_index in range(9):
        row_shift, col_shift = divmod(tap_index, 3)
        window_piece = padded[:, row_shift:row_shift + out_rows, col_shift:col_shift + out_cols].reshape(padded.shape[0], -1)
        running = running + jnp.dot(kernel[tap_index].T, window_piece, preferred_element_type=jnp.float32)
    return running

def back_taps(kernel, padded, out_rows, out_cols):
    running = jnp.zeros((kernel.shape[1], out_rows * out_cols), jnp.float32)
    for tap_index in range(9):
        row_shift, col_shift = divmod(tap_index, 3)
        window_piece = padded[:, 2 - row_shift:2 - row_shift + out_rows, 2 - col_shift:2 - col_shift + out_cols].reshape(padded.shape[0], -1)
        running = running + jnp.dot(kernel[tap_index], window_piece, preferred_element_type=jnp.float32)
    return running

def kernel_taps(padded, slope, out_rows, out_cols):
    grads = []
    for tap_index in range(9):
        row_shift, col_shift = divmod(tap_index, 3)
        window_piece = padded[:, row_shift:row_shift + out_rows, col_shift:col_shift + out_cols].reshape(padded.shape[0], -1)
        grads.append(lax.dot_general(window_piece, slope, (((1,), (1,)), ((), ())), preferred_element_type=jnp.float32))
    return jnp.stack(grads)

def contribute(pair):
    src_block, weight_block = pair
    return jnp.einsum('sfi,skij->skfj', src_block.astype(jnp.float32), weight_block.astype(jnp.float32)).astype(jnp.bfloat16)

def reference(source, intersection_weight, dest_tile, dest_row, prior_state, lift_weight, kernel, readout_weights):
    src_dev = source.reshape(DEVICES, S_DEV, QUANTITY_TOTAL, BLOCK)
    wts_dev = intersection_weight.reshape(DEVICES, S_DEV, K, BLOCK, BLOCK)
    contrib = lax.map(contribute, (src_dev, wts_dev))
    labels = (dest_tile * TB + dest_row).reshape(-1).astype(jnp.int32)
    blocks = jax.ops.segment_sum(contrib.reshape(-1, QUANTITY_TOTAL * BLOCK).astype(jnp.float32), labels, num_segments=DEVICES * TB)
    blocks = blocks.astype(jnp.bfloat16)
    remapped_reference = blocks.reshape(N_FACE, N_LON, ZONE_PARALLELS, W_DEV // BLOCK, QUANTITY_TOTAL, BLOCK)
    remapped_reference = remapped_reference.transpose(4, 0, 2, 1, 3, 5).reshape(QUANTITY_TOTAL, NLAT, MERIDIAN_TOTAL)
    objective_normalizer = 1.0 / math.sqrt(NLAT * MERIDIAN_TOTAL)
    state_pad = jnp.pad(prior_state, ((0, 0), (2, 2), (0, 0)))
    target_pad = jnp.pad(remapped_reference, ((0, 0), (2, 2), (0, 0)))
    valid_pad = jnp.pad(jnp.ones((NLAT,), jnp.float32), 2)

    def band_terms(band_index):
        band_start = (band_index * ZONE_PARALLELS).astype(jnp.int32)
        window = lax.dynamic_slice_in_dim(state_pad, band_start, ZONE_PARALLELS + 4, 1)
        valid_rows = lax.dynamic_slice_in_dim(valid_pad, band_start, ZONE_PARALLELS + 4, 0)
        reference_parallel_entries = lax.dynamic_slice_in_dim(target_pad, band_start + 1, ZONE_PARALLELS + 2, 1)
        lifted_wide = jnp.dot(lift_weight.T, window.reshape(QUANTITY_TOTAL, -1), preferred_element_type=jnp.float32)
        lifted_wide = lifted_wide.reshape(WIDTH, ZONE_PARALLELS + 4, MERIDIAN_TOTAL) * valid_rows[None, :, None]
        lifted = lifted_wide.astype(jnp.bfloat16)
        padded = wrap_lon(lifted)
        act = conv_taps(kernel, padded, ZONE_PARALLELS + 2, MERIDIAN_TOTAL)
        latent_activations = jax.nn.silu(act).astype(jnp.bfloat16)
        starting_condition = window[:, 1:ZONE_PARALLELS + 3].reshape(QUANTITY_TOTAL, -1).astype(jnp.float32)
        predicted_fields = starting_condition + jnp.dot(readout_weights.T, latent_activations, preferred_element_type=jnp.float32)
        predicted_fields = predicted_fields.reshape(QUANTITY_TOTAL, ZONE_PARALLELS + 2, MERIDIAN_TOTAL)
        parallel_cosine_factor = (objective_normalizer * valid_rows[1:ZONE_PARALLELS + 3])[None, :, None]
        prediction_mismatch = ((predicted_fields - reference_parallel_entries.astype(jnp.float32)) * parallel_cosine_factor).astype(jnp.bfloat16)
        latent_gradient = jnp.dot(readout_weights, prediction_mismatch.reshape(QUANTITY_TOTAL, -1), preferred_element_type=jnp.float32)
        sigmoid_act = jax.nn.sigmoid(act)
        slope = (latent_gradient * sigmoid_act * (1.0 + act * (1.0 - sigmoid_act))).astype(jnp.bfloat16)
        slope = slope.reshape(WIDTH, ZONE_PARALLELS + 2, MERIDIAN_TOTAL)
        hidden_band = latent_activations.reshape(WIDTH, ZONE_PARALLELS + 2, MERIDIAN_TOTAL)[:, 1:ZONE_PARALLELS + 1].reshape(WIDTH, -1)
        zone_residual = prediction_mismatch[:, 1:ZONE_PARALLELS + 1].reshape(QUANTITY_TOTAL, -1)
        slope_band = slope[:, 1:ZONE_PARALLELS + 1].reshape(WIDTH, -1)
        readout_term = lax.dot_general(hidden_band, zone_residual, (((1,), (1,)), ((), ())), preferred_element_type=jnp.float32)
        stencil_term = kernel_taps(padded[:, 1:], slope_band, ZONE_PARALLELS, MERIDIAN_TOTAL)
        lifted_grad = back_taps(kernel, wrap_lon(slope), ZONE_PARALLELS, MERIDIAN_TOTAL).astype(jnp.bfloat16)
        state_band = window[:, 2:ZONE_PARALLELS + 2].reshape(QUANTITY_TOTAL, -1)
        embedding_term = lax.dot_general(state_band, lifted_grad, (((1,), (1,)), ((), ())), preferred_element_type=jnp.float32)
        zone_prediction_slice = predicted_fields[:, 1:ZONE_PARALLELS + 1].astype(jnp.bfloat16)
        return (zone_prediction_slice, embedding_term, stencil_term, readout_term)
    bands, lift_terms, kernel_terms, head_terms = lax.map(band_terms, jnp.arange(N_FACE, dtype=jnp.int32))
    network_estimate = bands.transpose(1, 0, 2, 3).reshape(QUANTITY_TOTAL, NLAT, MERIDIAN_TOTAL)
    grad_lift = lax.optimization_barrier(jnp.sum(lift_terms, axis=0))
    grad_kernel = lax.optimization_barrier(jnp.sum(kernel_terms, axis=0))
    grad_head = lax.optimization_barrier(jnp.sum(head_terms, axis=0))
    return (remapped_reference, network_estimate, grad_lift, grad_kernel, grad_head)
```

```python
import functools

import jax
import jax.numpy as jnp
from jax import lax
from jax.experimental import pallas as pl
from jax.experimental.pallas import tpu as pltpu
from jax.sharding import PartitionSpec as P

MESH = pl.DeviceIdType.MESH
F32, BF16, I32 = jnp.float32, jnp.bfloat16, jnp.int32
N_FACE, N_LON = 8, 16
N_DEV = N_FACE * N_LON
NT = (((1,), (1,)), ((), ()))
WEIGHT_CHUNKS = 4


def mm(a, b):
    return jnp.dot(a, b, preferred_element_type=F32)


def nt(a, b):
    return lax.dot_general(a, b, NT, preferred_element_type=F32)


def rc(rows, cols):
    return (
        lax.broadcasted_iota(I32, (rows, cols), 0),
        lax.broadcasted_iota(I32, (rows, cols), 1),
    )


def onehot(mask):
    return jnp.where(mask, 1.0, 0.0).astype(BF16)


def peer(index):
    return (index // N_LON, index % N_LON)


def step_kernel(
    src_hbm, wts_hbm, tile_hbm, row_hbm, prior_hbm, lift_hbm, kern_hbm, read_hbm,
    rem_ref, est_ref, tot_ref,
    src, wts, dtile, drow, prior, lift, kern, read,
    contrib, idx_v, idx_s, lab_out, lab_in, send, recv,
    er_out, ec_out, er_in, ec_in, p3, l3, wconv, fore, hid, dsl, arr1, arr2, sum1,
    tbuf,
    in_sem, w_sem, idx_sem, lab_ss, lab_rs, pay_ss, pay_rs,
    halo_ss, halo_rs, ar_ss, ar1_rs, ar2_rs,
):
    face = lax.axis_index("face")
    lon = lax.axis_index("lon")
    me = face * N_LON + lon

    small = [
        (tile_hbm, dtile), (row_hbm, drow), (prior_hbm, prior), (src_hbm, src),
        (lift_hbm, lift), (kern_hbm, kern), (read_hbm, read),
    ]
    loads = [pltpu.make_async_copy(a, b, in_sem.at[i]) for i, (a, b) in enumerate(small)]
    for c in loads:
        c.start()
    per = 32 // WEIGHT_CHUNKS
    wloads = [
        pltpu.make_async_copy(
            wts_hbm.at[pl.ds(i * per, per)], wts.at[pl.ds(i * per, per)], w_sem.at[i]
        )
        for i in range(WEIGHT_CHUNKS)
    ]
    for c in wloads:
        c.start()

    barrier = pltpu.get_barrier_semaphore()

    def greet(i, carry):
        other = lax.rem(me + i, N_DEV)
        pl.semaphore_signal(barrier, inc=1, device_id=peer(other), device_id_type=MESH)
        return carry

    lax.fori_loop(1, N_DEV, greet, 0)
    for c in loads:
        c.wait()

    pr, ps = rc(128, 32)
    expand = onehot(pr // 4 == ps)
    dcol4 = mm(expand, dtile[...].astype(F32).astype(BF16))
    rcol4 = mm(expand, drow[...].astype(F32).astype(BF16))
    r4, c4 = rc(128, 4)
    pick = r4 % 4 == c4
    dcol = jnp.sum(jnp.where(pick, dcol4, 0.0), axis=1, keepdims=True)
    lcol = jnp.sum(jnp.where(pick, rcol4, 0.0), axis=1, keepdims=True)
    ri, ci = rc(128, 128)
    diag = jnp.where(ri == ci, jnp.broadcast_to(dcol, (128, 128)), 0.0)
    dlane = jnp.sum(diag, axis=0, keepdims=True)
    same = (jnp.broadcast_to(dcol, (128, 128)) == dlane) & (ci < ri)
    rank = jnp.sum(jnp.where(same, 1.0, 0.0), axis=1, keepdims=True)
    pos = 2.0 * dcol + rank
    r2, c2 = rc(128, 256)
    hit = jnp.broadcast_to(pos, (128, 256)) == c2.astype(F32)
    index = jnp.sum(jnp.where(hit, r2.astype(F32), 0.0), axis=0, keepdims=True)
    idx_v[...] = index.astype(I32)
    idx_copy = pltpu.make_async_copy(idx_v, idx_s, idx_sem)
    idx_copy.start()
    slot = ((ci // 8) % 2).astype(F32)
    labels = jnp.where(
        jnp.broadcast_to(rank, (128, 128)) == slot,
        jnp.broadcast_to(lcol, (128, 128)) + 1.0,
        0.0,
    ).astype(BF16)
    owners = onehot(jnp.broadcast_to(dlane, (128, 128)) == ri.astype(F32))
    code = mm(owners, labels) - 1.0
    code = jnp.where(code < 0.0, -1.0, code * 8.0 + (ci % 8).astype(F32)).astype(I32)
    lab_out[...] = code.reshape(128, 1, 128)
    lab_in[pl.ds(me, 1)] = lab_out[pl.ds(me, 1)]

    r, c = rc(256, 256)
    perm = onehot((r // 8 == c % 32) & (r % 8 == c // 32))
    shift0 = onehot(r == c - 1)
    shift2 = onehot(r == c + 1)
    eye = onehot(r == c)
    pf = mm(perm, prior[...].reshape(256, 256))
    pb = pf.astype(BF16)
    p3[1, pl.ds(16, 256), :] = pb
    er_out[...] = jnp.concatenate([pf[0:8], pf[248:256]], axis=0).astype(BF16)
    r16, c16 = rc(16, 256)
    edge = onehot(((r16 == 0) & (c16 == 0)) | ((r16 == 1) & (c16 == 255)))
    ec_out[...] = nt(edge, pb).astype(BF16)

    pl.semaphore_wait(barrier, N_DEV - 1)

    up, down = lax.rem(face + N_FACE - 1, N_FACE), lax.rem(face + 1, N_FACE)
    left, right = lax.rem(lon + N_LON - 1, N_LON), lax.rem(lon + 1, N_LON)
    halos = []
    ways = [(up, left), (up, lon), (up, right), (down, left), (down, lon), (down, right)]
    for k, (f, l) in enumerate(ways):
        halos.append(
            pltpu.make_async_remote_copy(
                er_out, er_in.at[5 - k], halo_ss.at[k], halo_rs.at[5 - k],
                device_id=(f, l), device_id_type=MESH,
            )
        )
    for k, l in enumerate((left, right)):
        halos.append(
            pltpu.make_async_remote_copy(
                ec_out, ec_in.at[1 - k], halo_ss.at[6 + k], halo_rs.at[7 - k],
                device_id=(face, l), device_id_type=MESH,
            )
        )
    for h in halos:
        h.start()

    def send_label(i, carry):
        other = lax.rem(me + i, N_DEV)
        pltpu.make_async_remote_copy(
            lab_out.at[other], lab_in.at[me], lab_ss, lab_rs,
            device_id=peer(other), device_id_type=MESH,
        ).start()
        return carry

    lax.fori_loop(1, N_DEV, send_label, 0)

    for chunk in range(WEIGHT_CHUNKS):
        wloads[chunk].wait()

        def regrid(s, carry):
            block = jnp.concatenate([wts[s, k] for k in range(4)], axis=1)
            out = mm(src[s], block)
            for k in range(4):
                contrib[s * 4 + k] = out[:, k * 128 : (k + 1) * 128].astype(BF16).astype(F32)
            return carry

        lax.fori_loop(chunk * per, (chunk + 1) * per, regrid, 0, unroll=4)
    idx_copy.wait()

    def place(d, carry):
        a = contrib[jnp.clip(idx_s[0, 2 * d], 0, 127)]
        b = contrib[jnp.clip(idx_s[0, 2 * d + 1], 0, 127)]
        send[d] = jnp.concatenate([a, b], axis=0).astype(BF16)
        return carry

    lax.fori_loop(0, N_DEV, place, 0, unroll=8)
    recv[pl.ds(me, 1)] = send[pl.ds(me, 1)]

    def send_block(i, carry):
        other = lax.rem(me + i, N_DEV)
        pltpu.make_async_remote_copy(
            send.at[other], recv.at[me], pay_ss, pay_rs,
            device_id=peer(other), device_id_type=MESH,
        ).start()
        return carry

    lax.fori_loop(1, N_DEV, send_block, 0)

    i64r, i64c = rc(128, 64)
    eye2 = onehot(i64r % 64 == i64c)
    liftf = lift[...].astype(F32)
    lift2 = jnp.concatenate([liftf, liftf], axis=0).astype(BF16)
    br, bc = rc(128, 16)
    block_mask = br // 64 == bc // 8
    bd_lift = jnp.where(block_mask, nt(eye2, lift2), 0.0).astype(BF16)
    read2 = jnp.concatenate([read[...], read[...]], axis=0)
    er8, ec8 = rc(8, 16)
    bd_read = jnp.where(block_mask, mm(read2, onehot(er8 == ec8 % 8)), 0.0).astype(BF16)
    fr8, fc8 = rc(16, 8)
    tr, tc = rc(16, 128)
    bd_read_t = jnp.where(
        tr // 8 == tc // 64, nt(onehot(fr8 % 8 == fc8), read2), 0.0
    ).astype(BF16)
    taps = kern[...].reshape(576, 64)
    zeros = jnp.zeros((192, 64), BF16)
    eye1 = eye2[0:64]
    wconv[0:64, :] = nt(eye1, jnp.concatenate([taps, zeros], axis=0)).astype(BF16)
    wconv[64:128, :] = nt(eye1, jnp.concatenate([zeros, taps], axis=0)).astype(BF16)

    for h in halos:
        h.wait()
    keep_up = jnp.where(face > 0, 1.0, 0.0)
    keep_down = jnp.where(face < N_FACE - 1, 1.0, 0.0)
    z8 = jnp.zeros((8, 256), F32)

    def rows_of(k):
        upper = er_in[k].astype(F32)[8:16] * keep_up
        lower = er_in[k + 3].astype(F32)[0:8] * keep_down
        return (
            jnp.concatenate([z8, upper], axis=0).astype(BF16),
            jnp.concatenate([lower, z8], axis=0).astype(BF16),
        )

    corner0 = onehot((r == 255) & (c == 0))
    corner2 = onehot((r == 0) & (c == 255))
    mid, lef, rig = rows_of(1), rows_of(0), rows_of(2)
    for at, e in ((0, 0), (272, 1)):
        p3[1, pl.ds(at, 16), :] = mid[e]
        p3[0, pl.ds(at, 16), :] = (mm(mid[e], shift0) + mm(lef[e], corner0)).astype(BF16)
        p3[2, pl.ds(at, 16), :] = (mm(mid[e], shift2) + mm(rig[e], corner2)).astype(BF16)
    col0 = onehot((r16 == 1) & (c16 == 0))
    col2 = onehot((r16 == 0) & (c16 == 255))
    from_left = nt(eye, ec_in[0]).astype(BF16)
    from_right = nt(eye, ec_in[1]).astype(BF16)
    p3[0, pl.ds(16, 256), :] = (mm(pb, shift0) + mm(from_left, col0)).astype(BF16)
    p3[2, pl.ds(16, 256), :] = (mm(pb, shift2) + mm(from_right, col2)).astype(BF16)

    def lift_pair(m, carry):
        at = pl.multiple_of(m * 16, 16)
        for j in range(3):
            out = mm(bd_lift, p3[j, pl.ds(at, 16), :]).astype(BF16)
            for e in range(2):
                to = pl.multiple_of((2 * m + e) * 192 + j * 64, 64)
                l3[pl.ds(to, 64), :] = out[e * 64 : (e + 1) * 64]
        return carry

    lax.fori_loop(0, 18, lift_pair, 0, unroll=2)

    def conv_pair(m, carry):
        at = pl.multiple_of((2 * m + 1) * 192, 64)
        act = mm(wconv[...], l3[pl.ds(at, 768), :])
        sig = 0.5 * jnp.tanh(0.5 * act) + 0.5
        hidden = (act * sig).astype(BF16)
        to = pl.multiple_of(m * 128, 128)
        hid[pl.ds(to, 128), :] = hidden
        dsl[pl.ds(to, 128), :] = sig * (1.0 + act * (1.0 - sig))
        row = pl.multiple_of(m * 16, 16)
        prow = pl.multiple_of(m * 16 + 16, 16)
        fore[pl.ds(row, 16), :] = p3[1, pl.ds(prow, 16), :].astype(F32) + mm(bd_read_t, hidden)
        return carry

    lax.fori_loop(0, 16, conv_pair, 0, unroll=2)
    perm_t = onehot((r // 32 == c % 8) & (r % 32 == c // 8))
    forecast = fore[...]
    est_ref[...] = mm(perm_t, forecast.astype(BF16)).astype(BF16).reshape(8, 32, 256)

    pltpu.make_async_copy(
        lab_in.at[pl.ds(0, N_DEV - 1)], lab_in.at[pl.ds(0, N_DEV - 1)], lab_rs
    ).wait()
    pltpu.make_async_copy(
        recv.at[pl.ds(0, N_DEV - 1)], recv.at[pl.ds(0, N_DEV - 1)], pay_rs
    ).wait()
    target = 16 * (r // 8) + r % 8
    halves = [jnp.zeros((256, 128), F32), jnp.zeros((256, 128), F32)]
    for t in range(8):
        lab = lab_in[pl.ds(16 * t, 16)].reshape(16, 128)
        lab = jnp.concatenate([lab, lab], axis=1)
        lane_code = jnp.sum(jnp.where(c16 // 16 == r16, lab, 0), axis=0, keepdims=True)
        lane_code = jnp.broadcast_to(lane_code, (256, 256))
        block = recv[pl.ds(16 * t, 16)].reshape(256, 128)
        for h in range(2):
            halves[h] = halves[h] + mm(onehot(lane_code == target + 8 * h), block)
    remap = jnp.concatenate(halves, axis=1).astype(BF16)
    rem_ref[...] = mm(perm_t, remap).astype(BF16).reshape(8, 32, 256)
    misfit = ((forecast - remap.astype(F32)) * (1.0 / 1024.0)).astype(BF16)
    fore[...] = misfit.astype(F32)

    def grad_pair(m, carry):
        head, accs = carry
        at = pl.multiple_of(m * 16, 16)
        to = pl.multiple_of(m * 128, 128)
        mis = fore[pl.ds(at, 16), :].astype(BF16)
        slope = (mm(bd_read, mis) * dsl[pl.ds(to, 128), :]).astype(BF16)
        head = head + nt(mis, hid[pl.ds(to, 128), :])
        accs = tuple(accs[j] + nt(p3[j, pl.ds(at, 48), :], slope) for j in range(3))
        return head, accs

    head, accs = lax.fori_loop(
        0, 16, grad_pair,
        (jnp.zeros((16, 128), F32), tuple(jnp.zeros((48, 128), F32) for _ in range(3))),
        unroll=2,
    )
    pairs = []
    for t in range(9):
        i, j = divmod(t, 3)
        pairs.append((accs[j][8 * i + 8 : 8 * i + 16], accs[j][8 * i + 16 : 8 * i + 24]))
    pairs.append((head[0:8], head[8:16]))
    low = lax.broadcasted_iota(I32, (8, 128), 1) < 64
    parts = []
    for b in range(5):
        a0, b0 = pairs[b]
        a1, b1 = pairs[b + 5]
        parts.append(
            jnp.where(low, a0 + pltpu.roll(b0, 64, 1), pltpu.roll(a1, 64, 1) + b1)
        )
    mine = jnp.concatenate(parts, axis=0)
    tbuf[...] = mine
    arr1[pl.ds(lon, 1)] = mine[None]

    def reduce_lon(i, carry):
        other = lax.rem(lon + i, N_LON)
        pltpu.make_async_remote_copy(
            tbuf, arr1.at[lon], ar_ss.at[0], ar1_rs,
            device_id=(face, other), device_id_type=MESH,
        ).start()
        return carry

    lax.fori_loop(1, N_LON, reduce_lon, 0)
    pltpu.make_async_copy(
        arr1.at[pl.ds(0, N_LON - 1)], arr1.at[pl.ds(0, N_LON - 1)], ar1_rs
    ).wait()
    total = arr1[0]
    for k in range(1, N_LON):
        total = total + arr1[k]
    sum1[...] = total
    arr2[pl.ds(face, 1)] = total[None]

    def reduce_face(i, carry):
        other = lax.rem(face + i, N_FACE)
        pltpu.make_async_remote_copy(
            sum1, arr2.at[face], ar_ss.at[1], ar2_rs,
            device_id=(other, lon), device_id_type=MESH,
        ).start()
        return carry

    lax.fori_loop(1, N_FACE, reduce_face, 0)
    pltpu.make_async_copy(
        arr2.at[pl.ds(0, N_FACE - 1)], arr2.at[pl.ds(0, N_FACE - 1)], ar2_rs
    ).wait()
    total = arr2[0]
    for k in range(1, N_FACE):
        total = total + arr2[k]
    tot_ref[...] = total

    pltpu.make_async_copy(
        lab_out.at[pl.ds(0, N_DEV - 1)], lab_out.at[pl.ds(0, N_DEV - 1)], lab_ss
    ).wait()
    pltpu.make_async_copy(
        send.at[pl.ds(0, N_DEV - 1)], send.at[pl.ds(0, N_DEV - 1)], pay_ss
    ).wait()
    pltpu.make_async_copy(
        arr1.at[pl.ds(0, N_LON - 1)], arr1.at[pl.ds(0, N_LON - 1)], ar_ss.at[0]
    ).wait()
    pltpu.make_async_copy(
        arr2.at[pl.ds(0, N_FACE - 1)], arr2.at[pl.ds(0, N_FACE - 1)], ar_ss.at[1]
    ).wait()


def final_kernel(tot, rem, est, lift, kern, rem_out, est_out, gl_out, gk_out, gh_out):
    rem_out[...] = rem[...]
    est_out[...] = est[...]

    def split(x):
        a = x.astype(BF16)
        x = x - a.astype(F32)
        b = x.astype(BF16)
        x = x - b.astype(F32)
        return a, b, x.astype(BF16)

    blocks = []
    for b in range(10):
        v = tot[(b % 5) * 8 : (b % 5) * 8 + 8, :]
        if b >= 5:
            v = pltpu.roll(v, 64, 1)
        parts = [p.astype(F32) for p in split(v)]
        parts.append(jnp.zeros((8, 128), F32))
        blocks.append(jnp.concatenate(parts, axis=0).astype(BF16)[:, 0:64])
    er, ec = rc(64, 64)
    eye = onehot(er == ec)
    liftf = lift[...].astype(F32)
    lift4 = jnp.concatenate([liftf] * 4, axis=0).astype(BF16)
    lift_t = nt(eye, lift4).astype(BF16)
    grad_lift = jnp.zeros((32, 64), F32)
    for t in range(9):
        gk_out[t] = mm(lift_t, blocks[t])
        grad_lift = grad_lift + nt(blocks[t], kern[t])
    gl_out[...] = grad_lift[0:8] + grad_lift[8:16] + grad_lift[16:24]
    sr, sc = rc(32, 8)
    head = nt(eye, blocks[9]).astype(BF16)
    gh_out[...] = mm(head, onehot(sr % 8 == sc))


def per_device(source, weight, dest_tile, dest_row, prior, lift, kern, read):
    any_spec = pl.BlockSpec(memory_space=pl.ANY)
    vmem = pl.BlockSpec(memory_space=pltpu.VMEM)
    V = pltpu.VMEM
    DMA = pltpu.SemaphoreType.DMA
    rem, est, tot = pl.pallas_call(
        step_kernel,
        out_shape=(
            jax.ShapeDtypeStruct((8, 32, 256), BF16),
            jax.ShapeDtypeStruct((8, 32, 256), BF16),
            jax.ShapeDtypeStruct((40, 128), F32),
        ),
        in_specs=[any_spec] * 8,
        out_specs=(vmem, vmem, vmem),
        scratch_shapes=[
            V((32, 8, 128), BF16), V((32, 4, 128, 128), BF16), V((32, 4), I32), V((32, 4), I32),
            V((8, 32, 256), BF16), V((8, 64), BF16), V((9, 64, 64), BF16), V((64, 8), BF16),
            V((128, 8, 128), F32), V((1, 256), I32), pltpu.SMEM((1, 256), I32),
            V((128, 1, 128), I32), V((128, 1, 128), I32),
            V((128, 16, 128), BF16), V((128, 16, 128), BF16),
            V((16, 256), BF16), V((16, 256), BF16), V((6, 16, 256), BF16), V((2, 16, 256), BF16),
            V((3, 288, 256), BF16), V((36 * 192, 256), BF16), V((128, 768), BF16),
            V((256, 256), F32), V((2048, 256), BF16), V((2048, 256), F32),
            V((16, 40, 128), F32), V((8, 40, 128), F32), V((40, 128), F32), V((40, 128), F32),
            DMA((7,)), DMA((WEIGHT_CHUNKS,)), DMA, DMA, DMA, DMA, DMA,
            DMA((8,)), DMA((8,)), DMA((2,)), DMA, DMA,
        ],
        compiler_params=pltpu.CompilerParams(
            collective_id=0, has_side_effects=True, vmem_limit_bytes=40 << 20
        ),
        name="step",
    )(source, weight, dest_tile, dest_row, prior, lift, kern, read)
    rem, est, gl, gk, gh = pl.pallas_call(
        final_kernel,
        out_shape=(
            jax.ShapeDtypeStruct((8, 32, 256), BF16),
            jax.ShapeDtypeStruct((8, 32, 256), BF16),
            jax.ShapeDtypeStruct((8, 64), F32),
            jax.ShapeDtypeStruct((9, 64, 64), F32),
            jax.ShapeDtypeStruct((64, 8), F32),
        ),
        in_specs=[vmem] * 5,
        out_specs=(vmem,) * 5,
        name="final",
    )(tot, rem, est, lift, kern)
    return rem, est, gl, gk, gh


def solution(mesh):
    return jax.shard_map(
        per_device,
        mesh=mesh,
        in_specs=(
            P(("face", "lon"), None, None),
            P(("face", "lon"), None, None, None),
            P(("face", "lon"), None),
            P(("face", "lon"), None),
            P(None, "face", "lon"),
            P(),
            P(),
            P(),
        ),
        out_specs=(P(None, "face", "lon"), P(None, "face", "lon"), P(), P(), P()),
        check_vma=False,
    )
```

```python
import jax
import jax.numpy as jnp
from jax import lax
from jax.experimental import pallas as pl
from jax.experimental.pallas import tpu as pltpu
from jax.sharding import PartitionSpec as P

MESH, LOGICAL = pl.DeviceIdType.MESH, pl.DeviceIdType.LOGICAL
F32, BF16, I32 = jnp.float32, jnp.bfloat16, jnp.int32
N_FACE, N_LON = 8, 16
N_DEV = N_FACE * N_LON
NT = (((1,), (1,)), ((), ()))
WEIGHT_CHUNKS = 4
LIFT_UNROLL, CONV_UNROLL, GRAD_UNROLL = 3, 2, 2


def mm(a, b):
    return jnp.dot(a, b, preferred_element_type=F32)


def nt(a, b):
    return lax.dot_general(a, b, NT, preferred_element_type=F32)


def rc(rows, cols):
    return (
        lax.broadcasted_iota(I32, (rows, cols), 0),
        lax.broadcasted_iota(I32, (rows, cols), 1),
    )


def onehot(mask):
    return jnp.where(mask, 1.0, 0.0).astype(BF16)


def step_kernel(
    src_hbm, wts_hbm, tile_hbm, row_hbm, prior_hbm, lift_hbm, kern_hbm, read_hbm,
    rem_ref, est_ref, tot_ref,
    src, wts, dtile, drow, prior, lift, kern, read,
    contrib, idx_v, idx_s, lab_out, lab_in, send, recv, wide,
    er_out, ec_out, er_in, ec_in, p3, l3, wconv, fore, mis_ref, hid, dsl, arr1, arr2, sum1,
    tbuf,
    in_sem, w_sem, idx_sem, lab_ss, lab_rs, pay_ss, pay_rs,
    halo_ss, halo_rs, ar_ss, ar1_rs, ar2_rs,
):
    face = lax.axis_index("face")
    lon = lax.axis_index("lon")
    me = face * N_LON + lon

    small = [
        (tile_hbm, dtile), (row_hbm, drow), (prior_hbm, prior), (src_hbm, src),
        (lift_hbm, lift), (kern_hbm, kern), (read_hbm, read),
    ]
    loads = [pltpu.make_async_copy(a, b, in_sem.at[i]) for i, (a, b) in enumerate(small)]
    for c in loads:
        c.start()
    per = 32 // WEIGHT_CHUNKS
    wloads = [
        pltpu.make_async_copy(
            wts_hbm.at[pl.ds(i * per, per)], wts.at[pl.ds(i * per, per)], w_sem.at[i]
        )
        for i in range(WEIGHT_CHUNKS)
    ]
    for c in wloads:
        c.start()

    barrier = pltpu.get_barrier_semaphore()

    def others(action):
        def one(other):
            other = jnp.where(other == N_DEV - 1, 0, other + 1)
            action(other)
            return other

        other = me
        for _ in range(7):
            other = one(other)

        def eight(i, other):
            for _ in range(8):
                other = one(other)
            return other

        lax.fori_loop(1, N_DEV // 8, eight, other)

    others(
        lambda other: pl.semaphore_signal(
            barrier, inc=1, device_id=other, device_id_type=LOGICAL
        )
    )
    for c in loads:
        c.wait()

    ri, ci = rc(128, 128)
    tiles, rows = dtile[...], drow[...]
    d_row = jnp.concatenate([tiles[k : k + 1] for k in range(4)], axis=1)
    l_row = jnp.concatenate([rows[k : k + 1] for k in range(4)], axis=1)
    d_mat = jnp.broadcast_to(d_row, (128, 128))
    d_col = d_mat.T
    rank = jnp.sum(jnp.where((d_col == d_mat) & (ri < ci), 1, 0), axis=0, keepdims=True)
    pos = jnp.broadcast_to(2 * d_row + rank, (128, 128)).T
    idx_v[...] = jnp.concatenate(
        [
            jnp.sum(jnp.where(pos == ci + at, ri, 0), axis=0, keepdims=True)
            for at in (0, 128)
        ],
        axis=1,
    )
    idx_copy = pltpu.make_async_copy(idx_v, idx_s, idx_sem)
    idx_copy.start()
    l_col = jnp.broadcast_to(l_row, (128, 128)).T
    labels = jnp.where(pos - 2 * d_col == ci % 2, l_col + 1, 0).astype(F32).astype(BF16)
    code = (mm(onehot(d_mat == ri), labels) - 1.0).astype(I32)
    lab_out[...] = code.reshape(128, 1, 128)
    lab_in[pl.ds(me, 1)] = lab_out[pl.ds(me, 1)]

    r, c = rc(256, 256)
    perm = onehot((r // 8 == c % 32) & (r % 8 == c // 32))
    shift0 = onehot(r == c - 1)
    shift2 = onehot(r == c + 1)
    eye = onehot(r == c)
    pf = mm(perm, prior[...].reshape(256, 256))
    pb = pf.astype(BF16)
    p3[1, pl.ds(16, 256), :] = pb
    er_out[...] = jnp.concatenate([pf[0:8], pf[248:256]], axis=0).astype(BF16)
    r16, c16 = rc(16, 256)
    edge = onehot(((r16 == 0) & (c16 == 0)) | ((r16 == 1) & (c16 == 255)))
    ec_out[...] = nt(edge, pb).astype(BF16)

    i64r, i64c = rc(128, 64)
    eye2 = onehot(i64r % 64 == i64c)
    liftf = lift[...].astype(F32)
    lift2 = jnp.concatenate([liftf, liftf], axis=0).astype(BF16)
    br, bc = rc(128, 16)
    block_mask = br // 64 == bc // 8
    bd_lift = jnp.where(block_mask, nt(eye2, lift2), 0.0).astype(BF16)
    readf = read[...].astype(F32)
    read2 = jnp.concatenate([readf, readf], axis=0).astype(BF16)
    bd_read = jnp.where(block_mask, nt(eye2, read2), 0.0).astype(BF16)
    tr, tc = rc(16, 128)
    bd_read_t = jnp.where(
        tr // 8 == tc // 64,
        jnp.concatenate([jnp.concatenate([readf, readf], axis=1)] * 2, axis=0),
        0.0,
    ).astype(BF16)
    taps = kern[...].reshape(576, 64)
    zeros = jnp.zeros((192, 64), BF16)
    eye1 = eye2[0:64]
    wconv[0:64, :] = nt(eye1, jnp.concatenate([taps, zeros], axis=0)).astype(BF16)
    wconv[64:128, :] = nt(eye1, jnp.concatenate([zeros, taps], axis=0)).astype(BF16)

    for chunk in range(WEIGHT_CHUNKS):
        wloads[chunk].wait()

        def regrid(s, carry):
            block = jnp.concatenate([wts[s, k] for k in range(4)], axis=1)
            out = mm(src[s], block)
            for k in range(4):
                contrib[k * 32 + s] = out[:, k * 128 : (k + 1) * 128].astype(BF16).astype(F32)
            return carry

        lax.fori_loop(chunk * per, (chunk + 1) * per, regrid, 0, unroll=4)
    idx_copy.wait()

    def place(d, carry):
        a = contrib[idx_s[0, 2 * d]]
        b = contrib[idx_s[0, 2 * d + 1]]
        send[d] = jnp.concatenate([a, b], axis=0).astype(BF16)
        return carry

    lax.fori_loop(0, N_DEV, place, 0, unroll=16)
    recv[pl.ds(me, 1)] = send[pl.ds(me, 1)]

    pl.semaphore_wait(barrier, N_DEV - 1)

    up, down = lax.rem(face + N_FACE - 1, N_FACE), lax.rem(face + 1, N_FACE)
    left, right = lax.rem(lon + N_LON - 1, N_LON), lax.rem(lon + 1, N_LON)
    halos = []
    ways = [(up, left), (up, lon), (up, right), (down, left), (down, lon), (down, right)]
    for k, (f, l) in enumerate(ways):
        halos.append(
            pltpu.make_async_remote_copy(
                er_out, er_in.at[5 - k], halo_ss.at[k], halo_rs.at[5 - k],
                device_id=(f, l), device_id_type=MESH,
            )
        )
    for k, l in enumerate((left, right)):
        halos.append(
            pltpu.make_async_remote_copy(
                ec_out, ec_in.at[1 - k], halo_ss.at[6 + k], halo_rs.at[7 - k],
                device_id=(face, l), device_id_type=MESH,
            )
        )
    for h in halos:
        h.start()

    def send_block(other):
        pltpu.make_async_remote_copy(
            send.at[other], recv.at[me], pay_ss, pay_rs,
            device_id=other, device_id_type=LOGICAL,
        ).start()
        pltpu.make_async_remote_copy(
            lab_out.at[other], lab_in.at[me], lab_ss, lab_rs,
            device_id=other, device_id_type=LOGICAL,
        ).start()

    others(send_block)

    for h in halos:
        h.wait()
    keep_up = jnp.where(face > 0, 1.0, 0.0)
    keep_down = jnp.where(face < N_FACE - 1, 1.0, 0.0)
    z8 = jnp.zeros((8, 256), F32)

    def rows_of(k):
        upper = er_in[k].astype(F32)[8:16] * keep_up
        lower = er_in[k + 3].astype(F32)[0:8] * keep_down
        return jnp.concatenate([z8, upper, lower, z8], axis=0).astype(BF16)

    corner0 = onehot((r == 255) & (c == 0))
    corner2 = onehot((r == 0) & (c == 255))
    mid, lef, rig = rows_of(1), rows_of(0), rows_of(2)
    outer0 = (mm(mid, shift0) + mm(lef, corner0)).astype(BF16)
    outer2 = (mm(mid, shift2) + mm(rig, corner2)).astype(BF16)
    for j, outer in ((0, outer0), (1, mid), (2, outer2)):
        p3[j, pl.ds(0, 16), :] = outer[0:16]
        p3[j, pl.ds(272, 16), :] = outer[16:32]
    col0 = onehot((r16 == 1) & (c16 == 0))
    col2 = onehot((r16 == 0) & (c16 == 255))
    pb = p3[1, pl.ds(16, 256), :]
    from_left = nt(eye, ec_in[0]).astype(BF16)
    from_right = nt(eye, ec_in[1]).astype(BF16)
    p3[0, pl.ds(16, 256), :] = (mm(pb, shift0) + mm(from_left, col0)).astype(BF16)
    p3[2, pl.ds(16, 256), :] = (mm(pb, shift2) + mm(from_right, col2)).astype(BF16)

    def lift_pair(m, carry):
        at = pl.multiple_of(m * 16, 16)
        for j in range(3):
            out = mm(bd_lift, p3[j, pl.ds(at, 16), :]).astype(BF16)
            for e in range(2):
                to = pl.multiple_of((2 * m + e) * 192 + j * 64, 64)
                l3[pl.ds(to, 64), :] = out[e * 64 : (e + 1) * 64]
        return carry

    lax.fori_loop(0, 18, lift_pair, 0, unroll=LIFT_UNROLL)

    def conv_pair(m, carry):
        at = pl.multiple_of((2 * m + 1) * 192, 64)
        act = mm(wconv[...], l3[pl.ds(at, 768), :])
        sig = 0.5 * jnp.tanh(0.5 * act) + 0.5
        hidden = (act * sig).astype(BF16)
        to = pl.multiple_of(m * 128, 128)
        hid[pl.ds(to, 128), :] = hidden
        dsl[pl.ds(to, 128), :] = sig * (1.0 + act * (1.0 - sig))
        row = pl.multiple_of(m * 16, 16)
        prow = pl.multiple_of(m * 16 + 16, 16)
        fore[pl.ds(row, 16), :] = p3[1, pl.ds(prow, 16), :].astype(F32) + mm(bd_read_t, hidden)
        return carry

    lax.fori_loop(0, 16, conv_pair, 0, unroll=CONV_UNROLL)
    perm_t = onehot((r // 32 == c % 8) & (r % 32 == c // 8))
    est_ref[...] = mm(perm_t, fore[...].astype(BF16)).astype(BF16).reshape(8, 32, 256)

    pltpu.make_async_copy(
        lab_in.at[pl.ds(0, N_DEV - 1)], lab_in.at[pl.ds(0, N_DEV - 1)], lab_rs
    ).wait()
    lab = lab_in[...].reshape(128, 128)
    lr, lc = rc(64, 128)
    mine_mask = lr == lc // 2
    lane_label = jnp.concatenate(
        [
            jnp.sum(jnp.where(mine_mask, lab[at : at + 64], 0), axis=0, keepdims=True)
            for at in (0, 64)
        ],
        axis=1,
    )
    hr, _ = rc(64, 256)
    picker = onehot(jnp.broadcast_to(lane_label, (64, 256)) == 2 * (hr % 32) + hr // 32)
    pltpu.make_async_copy(
        recv.at[pl.ds(0, N_DEV - 1)], recv.at[pl.ds(0, N_DEV - 1)], pay_rs
    ).wait()
    wide[...] = recv[...].reshape(2048, 128).astype(F32)
    fields = []
    for q in range(8):
        block = wide[pl.ds(q, 256, stride=8), :].astype(BF16)
        part = mm(picker, block)
        fields.append(jnp.concatenate([part[0:32], part[32:64]], axis=1).astype(BF16))
    for q in range(8):
        rem_ref[q] = fields[q]
    remap = mm(perm, jnp.concatenate(fields, axis=0))
    mis_ref[...] = ((fore[...] - remap) * (1.0 / 1024.0)).astype(BF16)

    def grad_pair(m, carry):
        head, acc = carry
        at = pl.multiple_of(m * 16, 16)
        to = pl.multiple_of(m * 128, 128)
        mis = mis_ref[pl.ds(at, 16), :]
        slope = (mm(bd_read, mis) * dsl[pl.ds(to, 128), :]).astype(BF16)
        head = head + nt(mis, hid[pl.ds(to, 128), :])
        window = jnp.concatenate([p3[j, pl.ds(at, 48), :] for j in range(3)], axis=0)
        return head, acc + nt(window, slope)

    head, acc = lax.fori_loop(
        0, 16, grad_pair,
        (jnp.zeros((16, 128), F32), jnp.zeros((144, 128), F32)),
        unroll=GRAD_UNROLL,
    )
    pairs = []
    for t in range(9):
        i, j = divmod(t, 3)
        at = 48 * j + 8 * i + 8
        pairs.append((acc[at : at + 8], acc[at + 8 : at + 16]))
    pairs.append((head[0:8], head[8:16]))
    low = lax.broadcasted_iota(I32, (8, 128), 1) < 64
    parts = []
    for b in range(5):
        a0, b0 = pairs[b]
        a1, b1 = pairs[b + 5]
        parts.append(
            jnp.where(low, a0 + pltpu.roll(b0, 64, 1), pltpu.roll(a1, 64, 1) + b1)
        )
    mine = jnp.concatenate(parts, axis=0)
    tbuf[...] = mine
    arr1[pl.ds(lon, 1)] = mine[None]
    for i in range(1, N_LON):
        pltpu.make_async_remote_copy(
            tbuf, arr1.at[lon], ar_ss.at[0], ar1_rs,
            device_id=(face, lax.rem(lon + i, N_LON)), device_id_type=MESH,
        ).start()
    pltpu.make_async_copy(
        arr1.at[pl.ds(0, N_LON - 1)], arr1.at[pl.ds(0, N_LON - 1)], ar1_rs
    ).wait()
    total = arr1[0]
    for k in range(1, N_LON):
        total = total + arr1[k]
    sum1[...] = total
    arr2[pl.ds(face, 1)] = total[None]
    for i in range(1, N_FACE):
        pltpu.make_async_remote_copy(
            sum1, arr2.at[face], ar_ss.at[1], ar2_rs,
            device_id=(lax.rem(face + i, N_FACE), lon), device_id_type=MESH,
        ).start()
    pltpu.make_async_copy(
        arr2.at[pl.ds(0, N_FACE - 1)], arr2.at[pl.ds(0, N_FACE - 1)], ar2_rs
    ).wait()
    total = arr2[0]
    for k in range(1, N_FACE):
        total = total + arr2[k]
    tot_ref[...] = total

    pltpu.make_async_copy(
        lab_out.at[pl.ds(0, N_DEV - 1)], lab_out.at[pl.ds(0, N_DEV - 1)], lab_ss
    ).wait()
    pltpu.make_async_copy(
        send.at[pl.ds(0, N_DEV - 1)], send.at[pl.ds(0, N_DEV - 1)], pay_ss
    ).wait()
    pltpu.make_async_copy(
        arr1.at[pl.ds(0, N_LON - 1)], arr1.at[pl.ds(0, N_LON - 1)], ar_ss.at[0]
    ).wait()
    pltpu.make_async_copy(
        arr2.at[pl.ds(0, N_FACE - 1)], arr2.at[pl.ds(0, N_FACE - 1)], ar_ss.at[1]
    ).wait()


def final_kernel(
    tot_any, rem_any, est_any, lift, kern, rem_out, est_out, gl_out, gk_out, gh_out, tot, sem
):
    moves = [
        pltpu.make_async_copy(tot_any, tot, sem.at[0]),
        pltpu.make_async_copy(rem_any, rem_out, sem.at[1]),
        pltpu.make_async_copy(est_any, est_out, sem.at[2]),
    ]
    for m in moves:
        m.start()
    moves[0].wait()

    def split(x):
        a = x.astype(BF16)
        x = x - a.astype(F32)
        b = x.astype(BF16)
        x = x - b.astype(F32)
        return a, b, x.astype(BF16)

    blocks = []
    for b in range(10):
        v = tot[(b % 5) * 8 : (b % 5) * 8 + 8, :]
        if b >= 5:
            v = pltpu.roll(v, 64, 1)
        if b == 9:
            gh_out[...] = v[:, 0:64]
            break
        parts = [p.astype(F32) for p in split(v)]
        parts.append(jnp.zeros((8, 128), F32))
        blocks.append(jnp.concatenate(parts, axis=0).astype(BF16)[:, 0:64])
    er, ec = rc(64, 64)
    eye = onehot(er == ec)
    liftf = lift[...].astype(F32)
    lift4 = jnp.concatenate([liftf] * 4, axis=0).astype(BF16)
    lift_t = nt(eye, lift4).astype(BF16)
    grad_lift = jnp.zeros((32, 64), F32)
    for t in range(9):
        gk_out[t] = mm(lift_t, blocks[t])
        grad_lift = grad_lift + nt(blocks[t], kern[t])
    gl_out[...] = grad_lift[0:8] + grad_lift[8:16] + grad_lift[16:24]
    moves[1].wait()
    moves[2].wait()


def per_device(source, weight, dest_tile, dest_row, prior, lift, kern, read):
    any_spec = pl.BlockSpec(memory_space=pl.ANY)
    hbm = pl.BlockSpec(memory_space=pltpu.HBM)
    vmem = pl.BlockSpec(memory_space=pltpu.VMEM)
    V = pltpu.VMEM
    DMA = pltpu.SemaphoreType.DMA
    rem, est, tot = pl.pallas_call(
        step_kernel,
        out_shape=(
            jax.ShapeDtypeStruct((8, 32, 256), BF16),
            jax.ShapeDtypeStruct((8, 32, 256), BF16),
            jax.ShapeDtypeStruct((40, 128), F32),
        ),
        in_specs=[hbm] * 8,
        out_specs=(vmem, vmem, vmem),
        scratch_shapes=[
            V((32, 8, 128), BF16), V((32, 4, 128, 128), BF16), V((4, 32), I32), V((4, 32), I32),
            V((8, 32, 256), BF16), V((8, 64), BF16), V((9, 64, 64), BF16), V((8, 64), BF16),
            V((128, 8, 128), F32), V((1, 256), I32), pltpu.SMEM((1, 256), I32),
            V((128, 1, 128), I32), V((128, 1, 128), I32),
            V((128, 16, 128), BF16), V((128, 16, 128), BF16), V((2048, 128), F32),
            V((16, 256), BF16), V((16, 256), BF16), V((6, 16, 256), BF16), V((2, 16, 256), BF16),
            V((3, 288, 256), BF16), V((36 * 192, 256), BF16), V((128, 768), BF16),
            V((256, 256), F32), V((256, 256), BF16), V((2048, 256), BF16), V((2048, 256), F32),
            V((16, 40, 128), F32), V((8, 40, 128), F32), V((40, 128), F32), V((40, 128), F32),
            DMA((7,)), DMA((WEIGHT_CHUNKS,)), DMA, DMA, DMA, DMA, DMA,
            DMA((8,)), DMA((8,)), DMA((2,)), DMA, DMA,
        ],
        compiler_params=pltpu.CompilerParams(
            collective_id=0, has_side_effects=True, vmem_limit_bytes=40 << 20
        ),
        name="step",
    )(*(
        pltpu.with_memory_space_constraint(x, pltpu.HBM)
        for x in (source, weight, dest_tile.T, dest_row.T, prior, lift, kern, read.T)
    ))
    rem, est, gl, gk, gh = pl.pallas_call(
        final_kernel,
        out_shape=(
            jax.ShapeDtypeStruct((8, 32, 256), BF16),
            jax.ShapeDtypeStruct((8, 32, 256), BF16),
            jax.ShapeDtypeStruct((8, 64), F32),
            jax.ShapeDtypeStruct((9, 64, 64), F32),
            jax.ShapeDtypeStruct((8, 64), F32),
        ),
        in_specs=[any_spec] * 3 + [vmem] * 2,
        out_specs=(hbm, hbm, vmem, vmem, vmem),
        scratch_shapes=[V((40, 128), F32), DMA((3,))],
        compiler_params=pltpu.CompilerParams(vmem_limit_bytes=16 << 20),
        name="final",
    )(tot, rem, est, lift, kern)
    return rem, est, gl, gk, gh.T


def solution(mesh):
    return jax.shard_map(
        per_device,
        mesh=mesh,
        in_specs=(
            P(("face", "lon"), None, None),
            P(("face", "lon"), None, None, None),
            P(("face", "lon"), None),
            P(("face", "lon"), None),
            P(None, "face", "lon"),
            P(),
            P(),
            P(),
        ),
        out_specs=(P(None, "face", "lon"), P(None, "face", "lon"), P(), P(), P()),
        check_vma=False,
    )
```

```python
import jax
import jax.numpy as jnp
from jax import lax
from jax.experimental import pallas as pl
from jax.experimental.pallas import tpu as pltpu
from jax.sharding import PartitionSpec as P

MESH, LOGICAL = pl.DeviceIdType.MESH, pl.DeviceIdType.LOGICAL
F32, BF16, I32 = jnp.float32, jnp.bfloat16, jnp.int32
N_FACE, N_LON = 8, 16
N_DEV = N_FACE * N_LON
NT = (((1,), (1,)), ((), ()))
WEIGHT_CHUNKS = 4
LIFT_UNROLL, CONV_UNROLL, GRAD_UNROLL = 3, 3, 8


def mm(a, b):
    return jnp.dot(a, b, preferred_element_type=F32)


def nt(a, b):
    return lax.dot_general(a, b, NT, preferred_element_type=F32)


def rc(rows, cols):
    return (
        lax.broadcasted_iota(I32, (rows, cols), 0),
        lax.broadcasted_iota(I32, (rows, cols), 1),
    )


def onehot(mask):
    return jnp.where(mask, 1.0, 0.0).astype(BF16)


def step_kernel(
    src_hbm, wts_hbm, tile_hbm, row_hbm, prior_hbm, lift_hbm, kern_hbm, read_hbm,
    rem_ref, est_ref, tot_ref,
    src, wts, dtile, drow, prior, lift, kern, read,
    contrib, idx_v, idx_s, lab_out, lab_in, send, recv, wide,
    er_out, ec_out, er_in, ec_in, p3, l3, wconv, fore, mis_ref, hid, dsl, acts, arr1, arr2, sum1,
    tbuf,
    in_sem, w_sem, idx_sem, lab_ss, lab_rs, pay_ss, pay_rs,
    halo_ss, halo_rs, ar_ss, ar1_rs, ar2_rs,
):
    face = lax.axis_index("face")
    lon = lax.axis_index("lon")
    me = face * N_LON + lon
    y, z = face // 2, lon // 4
    x = (face % 2) * 2 + (lon // 2) % 2
    core = lon % 2

    def at_xc(x_at, core_at):
        return (x_at // 2) * 16 + (x_at % 2) * 2 + core_at

    barrier = pltpu.get_barrier_semaphore()

    def others(action):
        zc = []
        for dz, dc in ((2, 1), (2, 0), (1, 1), (3, 1), (1, 0), (3, 0), (0, 1), (0, 0)):
            zc.append((lax.rem(z + dz, 4) * 4 + lax.rem(core + dc, 2), (dz, dc)))
        far = sorted(
            ((dy, dx) for dy in range(4) for dx in range(4)),
            key=lambda d: -(min(d[0], 4 - d[0]) + min(d[1], 4 - d[1])),
        )
        for dy, dx in far:
            base = lax.rem(y + dy, 4) * 32 + at_xc(lax.rem(x + dx, 4), 0)
            for offset, d in zc:
                if (dy, dx) + d != (0, 0, 0, 0):
                    action(base + offset)

    others(
        lambda other: pl.semaphore_signal(
            barrier, inc=1, device_id=other, device_id_type=LOGICAL
        )
    )
    small = [
        (tile_hbm, dtile), (row_hbm, drow), (prior_hbm, prior), (src_hbm, src),
        (lift_hbm, lift), (kern_hbm, kern), (read_hbm, read),
    ]
    loads = [pltpu.make_async_copy(a, b, in_sem.at[i]) for i, (a, b) in enumerate(small)]
    for c in loads:
        c.start()
    per = 32 // WEIGHT_CHUNKS
    wloads = [
        pltpu.make_async_copy(
            wts_hbm.at[pl.ds(i * per, per)], wts.at[pl.ds(i * per, per)], w_sem.at[i]
        )
        for i in range(WEIGHT_CHUNKS)
    ]
    for c in wloads:
        c.start()

    for c in loads:
        c.wait()

    ri, ci = rc(128, 128)
    tiles, rows = dtile[...], drow[...]
    d_row = jnp.concatenate([tiles[k : k + 1] for k in range(4)], axis=1)
    l_row = jnp.concatenate([rows[k : k + 1] for k in range(4)], axis=1)
    d_mat = jnp.broadcast_to(d_row, (128, 128))
    d_col = d_mat.T
    rank = jnp.sum(jnp.where((d_col == d_mat) & (ri < ci), 1, 0), axis=0, keepdims=True)
    pos = jnp.broadcast_to(2 * d_row + rank, (128, 128)).T
    idx_v[...] = jnp.concatenate(
        [
            jnp.sum(jnp.where(pos == ci + at, ri, 0), axis=0, keepdims=True)
            for at in (0, 128)
        ],
        axis=1,
    )
    idx_copy = pltpu.make_async_copy(idx_v, idx_s, idx_sem)
    idx_copy.start()
    l_col = jnp.broadcast_to(l_row, (128, 128)).T
    labels = jnp.where(pos - 2 * d_col == ci % 2, l_col + 1, 0).astype(F32).astype(BF16)
    code = (mm(onehot(d_mat == ri), labels) - 1.0).astype(I32)
    lab_out[...] = code.reshape(128, 1, 128)
    lab_in[pl.ds(me, 1)] = lab_out[pl.ds(me, 1)]

    r, c = rc(256, 256)
    perm = onehot((r // 8 == c % 32) & (r % 8 == c // 32))
    shift0 = onehot(r == c - 1)
    shift2 = onehot(r == c + 1)
    eye = onehot(r == c)
    pf = mm(perm, prior[...].reshape(256, 256))
    pb = pf.astype(BF16)
    p3[1, pl.ds(16, 256), :] = pb
    er_out[...] = jnp.concatenate([pf[0:8], pf[248:256]], axis=0).astype(BF16)
    r16, c16 = rc(16, 256)
    edge = onehot(((r16 == 0) & (c16 == 0)) | ((r16 == 1) & (c16 == 255)))
    ec_out[...] = nt(edge, pb).astype(BF16)

    i64r, i64c = rc(128, 64)
    eye2 = onehot(i64r % 64 == i64c)
    liftf = lift[...].astype(F32)
    lift2 = jnp.concatenate([liftf, liftf], axis=0).astype(BF16)
    br, bc = rc(128, 16)
    block_mask = br // 64 == bc // 8
    bd_lift = jnp.where(block_mask, nt(eye2, lift2), 0.0).astype(BF16)
    readf = read[...].astype(F32)
    read2 = jnp.concatenate([readf, readf], axis=0).astype(BF16)
    bd_read = jnp.where(block_mask, nt(eye2, read2), 0.0).astype(BF16)
    tr, tc = rc(16, 128)
    bd_read_t = jnp.where(
        tr // 8 == tc // 64,
        jnp.concatenate([jnp.concatenate([readf, readf], axis=1)] * 2, axis=0),
        0.0,
    ).astype(BF16)
    taps = kern[...].reshape(576, 64)
    zeros = jnp.zeros((192, 64), BF16)
    eye1 = eye2[0:64]
    wconv[0:64, :] = nt(eye1, jnp.concatenate([taps, zeros], axis=0)).astype(BF16)
    wconv[64:128, :] = nt(eye1, jnp.concatenate([zeros, taps], axis=0)).astype(BF16)

    for chunk in range(WEIGHT_CHUNKS):
        wloads[chunk].wait()

        def regrid(s, carry):
            block = jnp.concatenate([wts[s, k] for k in range(4)], axis=1)
            out = mm(src[s], block)
            for k in range(4):
                contrib[k * 32 + s] = out[:, k * 128 : (k + 1) * 128].astype(BF16).astype(F32)
            return carry

        lax.fori_loop(chunk * per, (chunk + 1) * per, regrid, 0, unroll=4)
    idx_copy.wait()

    def place(d, carry):
        a = contrib[idx_s[0, 2 * d]]
        b = contrib[idx_s[0, 2 * d + 1]]
        send[d] = jnp.concatenate([a, b], axis=0).astype(BF16)
        return carry

    lax.fori_loop(0, N_DEV, place, 0, unroll=16)
    recv[pl.ds(me, 1)] = send[pl.ds(me, 1)]

    pl.semaphore_wait(barrier, N_DEV - 1)

    up, down = lax.rem(face + N_FACE - 1, N_FACE), lax.rem(face + 1, N_FACE)
    left, right = lax.rem(lon + N_LON - 1, N_LON), lax.rem(lon + 1, N_LON)
    halos = []
    ways = [(up, left), (up, lon), (up, right), (down, left), (down, lon), (down, right)]
    for k, (f, l) in enumerate(ways):
        halos.append(
            pltpu.make_async_remote_copy(
                er_out, er_in.at[5 - k], halo_ss.at[k], halo_rs.at[5 - k],
                device_id=(f, l), device_id_type=MESH,
            )
        )
    for k, l in enumerate((left, right)):
        halos.append(
            pltpu.make_async_remote_copy(
                ec_out, ec_in.at[1 - k], halo_ss.at[6 + k], halo_rs.at[7 - k],
                device_id=(face, l), device_id_type=MESH,
            )
        )
    for h in halos:
        h.start()

    def send_block(other):
        pltpu.make_async_remote_copy(
            send.at[other], recv.at[me], pay_ss, pay_rs,
            device_id=other, device_id_type=LOGICAL,
        ).start()
        pltpu.make_async_remote_copy(
            lab_out.at[other], lab_in.at[me], lab_ss, lab_rs,
            device_id=other, device_id_type=LOGICAL,
        ).start()

    others(send_block)

    for h in halos:
        h.wait()
    keep_up = jnp.where(face > 0, 1.0, 0.0)
    keep_down = jnp.where(face < N_FACE - 1, 1.0, 0.0)
    z8 = jnp.zeros((8, 256), F32)

    def rows_of(k):
        upper = er_in[k].astype(F32)[8:16] * keep_up
        lower = er_in[k + 3].astype(F32)[0:8] * keep_down
        return jnp.concatenate([z8, upper, lower, z8], axis=0).astype(BF16)

    corner0 = onehot((r == 255) & (c == 0))
    corner2 = onehot((r == 0) & (c == 255))
    mid, lef, rig = rows_of(1), rows_of(0), rows_of(2)
    outer0 = (mm(mid, shift0) + mm(lef, corner0)).astype(BF16)
    outer2 = (mm(mid, shift2) + mm(rig, corner2)).astype(BF16)
    for j, outer in ((0, outer0), (1, mid), (2, outer2)):
        p3[j, pl.ds(0, 16), :] = outer[0:16]
        p3[j, pl.ds(272, 16), :] = outer[16:32]
    col0 = onehot((r16 == 1) & (c16 == 0))
    col2 = onehot((r16 == 0) & (c16 == 255))
    pb = p3[1, pl.ds(16, 256), :]
    from_left = nt(eye, ec_in[0]).astype(BF16)
    from_right = nt(eye, ec_in[1]).astype(BF16)
    p3[0, pl.ds(16, 256), :] = (mm(pb, shift0) + mm(from_left, col0)).astype(BF16)
    p3[2, pl.ds(16, 256), :] = (mm(pb, shift2) + mm(from_right, col2)).astype(BF16)

    def lift_pair(m, carry):
        at = pl.multiple_of(m * 16, 16)
        for j in range(3):
            out = mm(bd_lift, p3[j, pl.ds(at, 16), :]).astype(BF16)
            for e in range(2):
                to = pl.multiple_of((2 * m + e) * 192 + j * 64, 64)
                l3[pl.ds(to, 64), :] = out[e * 64 : (e + 1) * 64]
        return carry

    lax.fori_loop(0, 18, lift_pair, 0, unroll=LIFT_UNROLL)

    def conv_of(m):
        at = pl.multiple_of((2 * m + 1) * 192, 64)
        return mm(wconv[...], l3[pl.ds(at, 768), :])

    def activate(m, act):
        to = pl.multiple_of(m * 128, 128)
        row = pl.multiple_of(m * 16, 16)
        prow = pl.multiple_of(m * 16 + 16, 16)
        sig = 0.5 * jnp.tanh(0.5 * act) + 0.5
        value = act * sig
        hidden = value.astype(BF16)
        slope = sig + value * (1.0 - sig)
        increment = mm(bd_read_t, hidden)
        hid[pl.ds(to, 128), :] = hidden
        dsl[pl.ds(to, 128), :] = slope
        fore[pl.ds(row, 16), :] = p3[1, pl.ds(prow, 16), :].astype(F32) + increment

    def conv_pair(m, carry):
        before = acts[lax.rem(m + 1, 2)]
        act = conv_of(m)
        activate(m - 1, before)
        acts[lax.rem(m, 2)] = act
        return carry

    acts[0] = conv_of(0)
    lax.fori_loop(1, 16, conv_pair, 0, unroll=CONV_UNROLL)
    activate(15, acts[1])
    perm_t = onehot((r // 32 == c % 8) & (r % 32 == c // 8))
    est_ref[...] = mm(perm_t, fore[...].astype(BF16)).astype(BF16).reshape(8, 32, 256)

    pltpu.make_async_copy(
        lab_in.at[pl.ds(0, N_DEV - 1)], lab_in.at[pl.ds(0, N_DEV - 1)], lab_rs
    ).wait()
    lab = lab_in[...].reshape(128, 128)
    lr, lc = rc(64, 128)
    mine_mask = lr == lc // 2
    lane_label = jnp.concatenate(
        [
            jnp.sum(jnp.where(mine_mask, lab[at : at + 64], 0), axis=0, keepdims=True)
            for at in (0, 64)
        ],
        axis=1,
    )
    hr, _ = rc(64, 256)
    picker = onehot(jnp.broadcast_to(lane_label, (64, 256)) == 2 * (hr % 32) + hr // 32)
    pltpu.make_async_copy(
        recv.at[pl.ds(0, N_DEV - 1)], recv.at[pl.ds(0, N_DEV - 1)], pay_rs
    ).wait()
    wide[...] = recv[...].reshape(2048, 128).astype(F32)
    fields = []
    for q in range(8):
        block = wide[pl.ds(q, 256, stride=8), :].astype(BF16)
        part = mm(picker, block)
        fields.append(jnp.concatenate([part[0:32], part[32:64]], axis=1).astype(BF16))
    for q in range(8):
        rem_ref[q] = fields[q]
    remap = mm(perm, jnp.concatenate(fields, axis=0))
    mis_ref[...] = ((fore[...] - remap) * (1.0 / 1024.0)).astype(BF16)

    def grad_pair(m, carry):
        head, acc = carry
        at = pl.multiple_of(m * 16, 16)
        to = pl.multiple_of(m * 128, 128)
        mis = mis_ref[pl.ds(at, 16), :]
        slope = (mm(bd_read, mis) * dsl[pl.ds(to, 128), :]).astype(BF16)
        head = head + nt(mis, hid[pl.ds(to, 128), :])
        window = jnp.concatenate([p3[j, pl.ds(at, 48), :] for j in range(3)], axis=0)
        return head, acc + nt(window, slope)

    head, acc = lax.fori_loop(
        0, 16, grad_pair,
        (jnp.zeros((16, 128), F32), jnp.zeros((144, 128), F32)),
        unroll=GRAD_UNROLL,
    )
    pairs = []
    for t in range(9):
        i, j = divmod(t, 3)
        at = 48 * j + 8 * i + 8
        pairs.append((acc[at : at + 8], acc[at + 8 : at + 16]))
    pairs.append((head[0:8], head[8:16]))
    low = lax.broadcasted_iota(I32, (8, 128), 1) < 64
    parts = []
    for b in range(5):
        a0, b0 = pairs[b]
        a1, b1 = pairs[b + 5]
        parts.append(
            jnp.where(low, a0 + pltpu.roll(b0, 64, 1), pltpu.roll(a1, 64, 1) + b1)
        )
    mine = jnp.concatenate(parts, axis=0)
    tbuf[...] = mine
    group = x * 2 + core
    spot = y * 4 + z
    home = y * 32 + z * 4
    place_xc = at_xc(x, core)
    arr1[pl.ds(group, 1)] = mine[None]
    for k in (4, 5, 2, 3, 6, 7, 1):
        other = lax.rem(group + k, 8)
        pltpu.make_async_remote_copy(
            tbuf, arr1.at[group], ar_ss.at[0], ar1_rs,
            device_id=home + at_xc(other // 2, other % 2), device_id_type=LOGICAL,
        ).start()
    pltpu.make_async_copy(arr1.at[pl.ds(0, 7)], arr1.at[pl.ds(0, 7)], ar1_rs).wait()
    total = arr1[0]
    for k in range(1, 8):
        total = total + arr1[k]
    sum1[...] = total
    arr2[pl.ds(spot, 1)] = total[None]
    ring = sorted(
        ((dy, dz) for dy in range(4) for dz in range(4)),
        key=lambda d: -(min(d[0], 4 - d[0]) + min(d[1], 4 - d[1])),
    )
    for dy, dz in ring[:-1]:
        pltpu.make_async_remote_copy(
            sum1, arr2.at[spot], ar_ss.at[1], ar2_rs,
            device_id=lax.rem(y + dy, 4) * 32 + lax.rem(z + dz, 4) * 4 + place_xc,
            device_id_type=LOGICAL,
        ).start()
    pltpu.make_async_copy(arr2.at[pl.ds(0, 15)], arr2.at[pl.ds(0, 15)], ar2_rs).wait()
    total = arr2[0]
    for k in range(1, 16):
        total = total + arr2[k]
    tot_ref[...] = total

    pltpu.make_async_copy(
        lab_out.at[pl.ds(0, N_DEV - 1)], lab_out.at[pl.ds(0, N_DEV - 1)], lab_ss
    ).wait()
    pltpu.make_async_copy(
        send.at[pl.ds(0, N_DEV - 1)], send.at[pl.ds(0, N_DEV - 1)], pay_ss
    ).wait()
    pltpu.make_async_copy(
        arr1.at[pl.ds(0, 7)], arr1.at[pl.ds(0, 7)], ar_ss.at[0]
    ).wait()
    pltpu.make_async_copy(
        arr2.at[pl.ds(0, 15)], arr2.at[pl.ds(0, 15)], ar_ss.at[1]
    ).wait()


def final_kernel(
    tot_any, rem_any, est_any, lift, kern, rem_out, est_out, gl_out, gk_out, gh_out, tot, sem
):
    moves = [
        pltpu.make_async_copy(tot_any, tot, sem.at[0]),
        pltpu.make_async_copy(rem_any, rem_out, sem.at[1]),
        pltpu.make_async_copy(est_any, est_out, sem.at[2]),
    ]
    for m in moves:
        m.start()
    moves[0].wait()

    def split(x):
        a = x.astype(BF16)
        x = x - a.astype(F32)
        b = x.astype(BF16)
        x = x - b.astype(F32)
        return a, b, x.astype(BF16)

    blocks = []
    for b in range(10):
        v = tot[(b % 5) * 8 : (b % 5) * 8 + 8, :]
        if b >= 5:
            v = pltpu.roll(v, 64, 1)
        if b == 9:
            gh_out[...] = v[:, 0:64]
            break
        parts = [p.astype(F32) for p in split(v)]
        parts.append(jnp.zeros((8, 128), F32))
        blocks.append(jnp.concatenate(parts, axis=0).astype(BF16)[:, 0:64])
    er, ec = rc(64, 64)
    eye = onehot(er == ec)
    liftf = lift[...].astype(F32)
    lift4 = jnp.concatenate([liftf] * 4, axis=0).astype(BF16)
    lift_t = nt(eye, lift4).astype(BF16)
    grad_lift = jnp.zeros((32, 64), F32)
    for t in range(9):
        gk_out[t] = mm(lift_t, blocks[t])
        grad_lift = grad_lift + nt(blocks[t], kern[t])
    gl_out[...] = grad_lift[0:8] + grad_lift[8:16] + grad_lift[16:24]
    moves[1].wait()
    moves[2].wait()


def per_device(source, weight, dest_tile, dest_row, prior, lift, kern, read):
    any_spec = pl.BlockSpec(memory_space=pl.ANY)
    hbm = pl.BlockSpec(memory_space=pltpu.HBM)
    vmem = pl.BlockSpec(memory_space=pltpu.VMEM)
    V = pltpu.VMEM
    DMA = pltpu.SemaphoreType.DMA
    rem, est, tot = pl.pallas_call(
        step_kernel,
        out_shape=(
            jax.ShapeDtypeStruct((8, 32, 256), BF16),
            jax.ShapeDtypeStruct((8, 32, 256), BF16),
            jax.ShapeDtypeStruct((40, 128), F32),
        ),
        in_specs=[hbm] * 8,
        out_specs=(vmem, vmem, vmem),
        scratch_shapes=[
            V((32, 8, 128), BF16), V((32, 4, 128, 128), BF16), V((4, 32), I32), V((4, 32), I32),
            V((8, 32, 256), BF16), V((8, 64), BF16), V((9, 64, 64), BF16), V((8, 64), BF16),
            V((128, 8, 128), F32), V((1, 256), I32), pltpu.SMEM((1, 256), I32),
            V((128, 1, 128), I32), V((128, 1, 128), I32),
            V((128, 16, 128), BF16), V((128, 16, 128), BF16), V((2048, 128), F32),
            V((16, 256), BF16), V((16, 256), BF16), V((6, 16, 256), BF16), V((2, 16, 256), BF16),
            V((3, 288, 256), BF16), V((36 * 192, 256), BF16), V((128, 768), BF16),
            V((256, 256), F32), V((256, 256), BF16), V((2048, 256), BF16), V((2048, 256), F32),
            V((2, 128, 256), F32), V((8, 40, 128), F32), V((16, 40, 128), F32), V((40, 128), F32), V((40, 128), F32),
            DMA((7,)), DMA((WEIGHT_CHUNKS,)), DMA, DMA, DMA, DMA, DMA,
            DMA((8,)), DMA((8,)), DMA((2,)), DMA, DMA,
        ],
        compiler_params=pltpu.CompilerParams(
            collective_id=0, has_side_effects=True, vmem_limit_bytes=40 << 20
        ),
        name="step",
    )(*(
        pltpu.with_memory_space_constraint(x, pltpu.HBM)
        for x in (source, weight, dest_tile.T, dest_row.T, prior, lift, kern, read.T)
    ))
    rem, est, gl, gk, gh = pl.pallas_call(
        final_kernel,
        out_shape=(
            jax.ShapeDtypeStruct((8, 32, 256), BF16),
            jax.ShapeDtypeStruct((8, 32, 256), BF16),
            jax.ShapeDtypeStruct((8, 64), F32),
            jax.ShapeDtypeStruct((9, 64, 64), F32),
            jax.ShapeDtypeStruct((8, 64), F32),
        ),
        in_specs=[any_spec] * 3 + [vmem] * 2,
        out_specs=(hbm, hbm, vmem, vmem, vmem),
        scratch_shapes=[V((40, 128), F32), DMA((3,))],
        compiler_params=pltpu.CompilerParams(vmem_limit_bytes=16 << 20),
        name="final",
    )(tot, rem, est, lift, kern)
    return rem, est, gl, gk, gh.T


def solution(mesh):
    return jax.shard_map(
        per_device,
        mesh=mesh,
        in_specs=(
            P(("face", "lon"), None, None),
            P(("face", "lon"), None, None, None),
            P(("face", "lon"), None),
            P(("face", "lon"), None),
            P(None, "face", "lon"),
            P(),
            P(),
            P(),
        ),
        out_specs=(P(None, "face", "lon"), P(None, "face", "lon"), P(), P(), P()),
        check_vma=False,
    )
```

```python
import jax
import jax.numpy as jnp
from jax import lax
from jax.experimental import pallas as pl
from jax.experimental.pallas import tpu as pltpu
from jax.sharding import PartitionSpec as P

MESH, LOGICAL = pl.DeviceIdType.MESH, pl.DeviceIdType.LOGICAL
F32, BF16, I32 = jnp.float32, jnp.bfloat16, jnp.int32
N_FACE, N_LON = 8, 16
N_DEV = N_FACE * N_LON
NT = (((1,), (1,)), ((), ()))
WEIGHT_CHUNKS = 4
CONV_UNROLL, GRAD_UNROLL = 16, 16


def mm(a, b):
    return jnp.dot(a, b, preferred_element_type=F32)


def nt(a, b):
    return lax.dot_general(a, b, NT, preferred_element_type=F32)


def rc(rows, cols):
    return (
        lax.broadcasted_iota(I32, (rows, cols), 0),
        lax.broadcasted_iota(I32, (rows, cols), 1),
    )


def onehot(mask):
    return jnp.where(mask, 1.0, 0.0).astype(BF16)


FAR_FIRST = sorted(
    [
        (dy, dx, dz, dc)
        for dy in range(4) for dx in range(4) for dz in range(4) for dc in range(2)
    ][1:],
    key=lambda d: -sum(min(v, 4 - v) for v in d[:3]),
)


def step_kernel(
    src_hbm, wts_hbm, tile_hbm, row_hbm, prior_hbm, lift_hbm, kern_hbm, read_hbm,
    rem_ref, est_ref, tot_ref,
    src, wts, dtile, drow, prior, lift, kern, read,
    contrib, idx_v, idx_s, lab1_out, lab1_in, lab2_out, lab2_in, send, recv, wide,
    er_out, ec_out, er_in, ec_in, p3, l3, wconv, fore, mis_ref, hid, dsl, edges, arr1, arr2, sum1,
    tbuf,
    in_sem, w_sem, idx_sem, lab_ss, lab_rs, pay_ss, pay_rs,
    halo_ss, halo_rs, ar_ss, ar1_rs, ar2_rs,
):
    face = lax.axis_index("face")
    lon = lax.axis_index("lon")
    me = face * N_LON + lon
    y, z = face // 2, lon // 4
    x = (face % 2) * 2 + (lon // 2) % 2
    core = lon % 2
    group, spot = x * 2 + core, y * 4 + z
    home = y * 32 + z * 4
    here = spot * 8 + group

    def at_xc(x_at, core_at):
        return (x_at // 2) * 16 + (x_at % 2) * 2 + core_at

    barrier = pltpu.get_barrier_semaphore()

    y_at = [lax.rem(y + d, 4) * 32 for d in range(4)]
    x_at = [at_xc(lax.rem(x + d, 4), 0) for d in range(4)]
    zc_at = [lax.rem(z + d // 2, 4) * 4 + lax.rem(core + d % 2, 2) for d in range(8)]

    def others(action):
        for dy, dx, dz, dc in FAR_FIRST:
            action(y_at[dy] + x_at[dx] + zc_at[2 * dz + dc])

    others(
        lambda other: pl.semaphore_signal(
            barrier, inc=1, device_id=other, device_id_type=LOGICAL
        )
    )
    small = [
        (tile_hbm, dtile), (row_hbm, drow), (prior_hbm, prior), (src_hbm, src),
        (lift_hbm, lift), (kern_hbm, kern), (read_hbm, read),
    ]
    loads = [pltpu.make_async_copy(a, b, in_sem.at[i]) for i, (a, b) in enumerate(small)]
    for c in loads:
        c.start()
    per = 32 // WEIGHT_CHUNKS
    wloads = [
        pltpu.make_async_copy(
            wts_hbm.at[pl.ds(i * per, per)], wts.at[pl.ds(i * per, per)], w_sem.at[i]
        )
        for i in range(WEIGHT_CHUNKS)
    ]
    for c in wloads:
        c.start()

    for c in loads:
        c.wait()

    ri, ci = rc(128, 128)
    tiles, rows = dtile[...], drow[...]
    d_row = jnp.concatenate([tiles[k : k + 1] for k in range(4)], axis=1)
    l_row = jnp.concatenate([rows[k : k + 1] for k in range(4)], axis=1)
    d_mat = jnp.broadcast_to(d_row, (128, 128))
    d_col = d_mat.T
    rank = jnp.sum(jnp.where((d_col == d_mat) & (ri < ci), 1, 0), axis=0, keepdims=True)
    pos = jnp.broadcast_to(2 * d_row + rank, (128, 128)).T
    idx_v[...] = jnp.concatenate(
        [
            jnp.sum(jnp.where(pos == ci + at, ri, 0), axis=0, keepdims=True)
            for at in (0, 128)
        ],
        axis=1,
    )
    idx_copy = pltpu.make_async_copy(idx_v, idx_s, idx_sem)
    idx_copy.start()
    l_col = jnp.broadcast_to(l_row, (128, 128)).T
    spots = (d_col // 32) * 4 + (d_col // 4) % 4
    labels = jnp.where(spots * 2 + pos - 2 * d_col == ci, l_col + 1, 0).astype(F32).astype(BF16)
    d_few = d_mat[0:16]
    owners = onehot(((d_few // 16) % 2) * 4 + d_few % 4 == ri[0:16])
    lab1_out[...] = mm(owners, labels)[0:8].astype(I32).reshape(8, 1, 128)
    lab1_in[pl.ds(group, 1)] = lab1_out[pl.ds(group, 1)]

    r, c = rc(256, 256)
    perm = onehot((r // 8 == c % 32) & (r % 8 == c // 32))
    shift0 = onehot(r == c - 1)
    shift2 = onehot(r == c + 1)
    eye = onehot(r == c)
    pf = mm(perm, prior[...].reshape(256, 256))
    pb = pf.astype(BF16)
    p3[1, pl.ds(16, 256), :] = pb
    er_out[...] = jnp.concatenate([pf[0:8], pf[248:256]], axis=0).astype(BF16)
    r16, c16 = rc(16, 256)
    edge = onehot(((r16 == 0) & (c16 == 0)) | ((r16 == 1) & (c16 == 255)))
    ec_out[...] = nt(edge, pb).astype(BF16)

    for chunk in range(WEIGHT_CHUNKS):
        wloads[chunk].wait()

        def regrid(s, carry):
            block = jnp.concatenate([wts[s, k] for k in range(4)], axis=1)
            out = mm(src[s], block)
            for k in range(4):
                contrib[k * 32 + s] = out[:, k * 128 : (k + 1) * 128].astype(BF16).astype(F32)
            return carry

        lax.fori_loop(chunk * per, (chunk + 1) * per, regrid, 0, unroll=per)
    idx_copy.wait()

    def place(d, carry):
        a = contrib[idx_s[0, 2 * d]]
        b = contrib[idx_s[0, 2 * d + 1]]
        send[d] = jnp.concatenate([a, b], axis=0).astype(BF16)
        return carry

    lax.fori_loop(0, N_DEV, place, 0, unroll=16)
    recv[pl.ds(here, 1)] = send[pl.ds(me, 1)]

    pl.semaphore_wait(barrier, N_DEV - 1)

    up, down = lax.rem(face + N_FACE - 1, N_FACE), lax.rem(face + 1, N_FACE)
    left, right = lax.rem(lon + N_LON - 1, N_LON), lax.rem(lon + 1, N_LON)
    halos = []
    ways = [(up, left), (up, lon), (up, right), (down, left), (down, lon), (down, right)]
    for k, (f, l) in enumerate(ways):
        halos.append(
            pltpu.make_async_remote_copy(
                er_out, er_in.at[5 - k], halo_ss.at[k], halo_rs.at[5 - k],
                device_id=(f, l), device_id_type=MESH,
            )
        )
    for k, l in enumerate((left, right)):
        halos.append(
            pltpu.make_async_remote_copy(
                ec_out, ec_in.at[1 - k], halo_ss.at[6 + k], halo_rs.at[7 - k],
                device_id=(face, l), device_id_type=MESH,
            )
        )
    for h in halos:
        h.start()
    for k in (4, 5, 2, 3, 6, 7, 1):
        other = lax.rem(group + k, 8)
        pltpu.make_async_remote_copy(
            lab1_out.at[other], lab1_in.at[group], lab_ss.at[0], lab_rs.at[0],
            device_id=home + at_xc(other // 2, other % 2), device_id_type=LOGICAL,
        ).start()

    i64r, i64c = rc(128, 64)
    eye2 = onehot(i64r % 64 == i64c)
    liftf = lift[...].astype(F32)
    lift2 = jnp.concatenate([liftf, liftf], axis=0).astype(BF16)
    br, bc = rc(128, 16)
    block_mask = br // 64 == bc // 8
    bd_lift = jnp.where(block_mask, nt(eye2, lift2), 0.0).astype(BF16)
    readf = read[...].astype(F32)
    read2 = jnp.concatenate([readf, readf], axis=0).astype(BF16)
    bd_read = jnp.where(block_mask, nt(eye2, read2), 0.0).astype(BF16)
    tr, tc = rc(16, 128)
    bd_read_t = jnp.where(
        tr // 8 == tc // 64,
        jnp.concatenate([jnp.concatenate([readf, readf], axis=1)] * 2, axis=0),
        0.0,
    ).astype(BF16)
    taps = kern[...].reshape(576, 64)
    zeros = jnp.zeros((192, 64), BF16)
    eye1 = eye2[0:64]
    wconv[0:64, :] = nt(eye1, jnp.concatenate([taps, zeros], axis=0)).astype(BF16)
    wconv[64:128, :] = nt(eye1, jnp.concatenate([zeros, taps], axis=0)).astype(BF16)

    p3[0, pl.ds(16, 256), :] = mm(pb, shift0).astype(BF16)
    p3[2, pl.ds(16, 256), :] = mm(pb, shift2).astype(BF16)

    def lift_pair(m, carry):
        at = pl.multiple_of(m * 16, 16)
        for j in range(3):
            out = mm(bd_lift, p3[j, pl.ds(at, 16), :]).astype(BF16)
            for e in range(2):
                to = pl.multiple_of((2 * m + e) * 192 + j * 64, 64)
                l3[pl.ds(to, 64), :] = out[e * 64 : (e + 1) * 64]
        return carry

    def send_block(other):
        pltpu.make_async_remote_copy(
            send.at[other], recv.at[here], pay_ss, pay_rs,
            device_id=other, device_id_type=LOGICAL,
        ).start()

    others(send_block)
    for m in range(1, 17):
        lift_pair(m, 0)

    pltpu.make_async_copy(lab1_in.at[pl.ds(0, 7)], lab1_in.at[pl.ds(0, 7)], lab_rs.at[0]).wait()
    came = lab1_in[...].reshape(8, 128).astype(F32).astype(BF16)
    vr, vc = rc(128, 8)
    spread = mm(onehot((vr % 16) // 2 == vc), came)
    spread = jnp.where(ri % 2 == ci % 2, spread, 0.0).astype(BF16)
    lab2_out[...] = (
        nt(onehot(ri[0:16] == ci[0:16] // 2), spread).astype(I32).reshape(16, 1, 128)
    )
    lab2_in[pl.ds(spot, 1)] = lab2_out[pl.ds(spot, 1)]
    place_xc = at_xc(x, core)
    ring = sorted(
        ((dy, dz) for dy in range(4) for dz in range(4)),
        key=lambda d: -(min(d[0], 4 - d[0]) + min(d[1], 4 - d[1])),
    )[:-1]

    def in_ring(dy, dz):
        there_y, there_z = lax.rem(y + dy, 4), lax.rem(z + dz, 4)
        return there_y * 4 + there_z, there_y * 32 + there_z * 4 + place_xc

    for dy, dz in ring:
        other, device = in_ring(dy, dz)
        pltpu.make_async_remote_copy(
            lab2_out.at[other], lab2_in.at[spot], lab_ss.at[1], lab_rs.at[1],
            device_id=device, device_id_type=LOGICAL,
        ).start()

    for h in halos:
        h.wait()
    keep_up = jnp.where(face > 0, 1.0, 0.0)
    keep_down = jnp.where(face < N_FACE - 1, 1.0, 0.0)
    z8 = jnp.zeros((8, 256), F32)

    def rows_of(k):
        upper = er_in[k].astype(F32)[8:16] * keep_up
        lower = er_in[k + 3].astype(F32)[0:8] * keep_down
        return jnp.concatenate([z8, upper, lower, z8], axis=0).astype(BF16)

    corner0 = onehot((r == 255) & (c == 0))
    corner2 = onehot((r == 0) & (c == 255))
    mid, lef, rig = rows_of(1), rows_of(0), rows_of(2)
    outer0 = (mm(mid, shift0) + mm(lef, corner0)).astype(BF16)
    outer2 = (mm(mid, shift2) + mm(rig, corner2)).astype(BF16)
    for j, outer in ((0, outer0), (1, mid), (2, outer2)):
        p3[j, pl.ds(0, 16), :] = outer[0:16]
        p3[j, pl.ds(272, 16), :] = outer[16:32]
    halo_cols = []
    for e, (keep, src_row, lane) in enumerate(((ec_in[0], 1, 0), (ec_in[1], 0, 127))):
        sel = onehot((c16[:, 0:128] == lane) & (r16[:, 0:128] == src_row))
        halo_cols.append(mm(nt(eye, keep).astype(BF16), sel).astype(BF16))
        p3[2 * e, pl.ds(16, 256), pl.ds(128 * e, 128)] = (
            p3[2 * e, pl.ds(16, 256), pl.ds(128 * e, 128)] + halo_cols[e]
        )
        edges[e] = halo_cols[e]

    for m in (0, 17):
        lift_pair(m, 0)

    def lift_edges(m, carry):
        at = pl.multiple_of(m * 16, 16)
        for e in range(2):
            out = mm(bd_lift, edges[e, pl.ds(at, 16), :]).astype(BF16)
            for k in range(2):
                to = pl.multiple_of((2 * m + 2 + k) * 192 + 128 * e, 64)
                l3[pl.ds(to, 64), pl.ds(128 * e, 128)] = (
                    l3[pl.ds(to, 64), pl.ds(128 * e, 128)] + out[k * 64 : (k + 1) * 64]
                )
        return carry

    lax.fori_loop(0, 16, lift_edges, 0, unroll=4)

    def conv_of(m):
        at = pl.multiple_of((2 * m + 1) * 192, 64)
        return mm(wconv[...], l3[pl.ds(at, 768), :])

    def activate(m, act):
        to = pl.multiple_of(m * 128, 128)
        sig = 0.5 * jnp.tanh(0.5 * act) + 0.5
        value = act * sig
        hid[pl.ds(to, 128), :] = value.astype(BF16)
        dsl[pl.ds(to, 128), :] = sig + value * (1.0 - sig)

    def conv_pair(m, carry):
        activate(m, conv_of(m))
        return carry

    lax.fori_loop(0, 16, conv_pair, 0, unroll=CONV_UNROLL)

    def read_pair(m, carry):
        to = pl.multiple_of(m * 128, 128)
        row = pl.multiple_of(m * 16, 16)
        prow = pl.multiple_of(m * 16 + 16, 16)
        fore[pl.ds(row, 16), :] = p3[1, pl.ds(prow, 16), :].astype(F32) + mm(
            bd_read_t, hid[pl.ds(to, 128), :]
        )
        return carry

    lax.fori_loop(0, 16, read_pair, 0, unroll=4)
    perm_t = onehot((r // 32 == c % 8) & (r % 32 == c // 8))
    est_ref[...] = mm(perm_t, fore[...].astype(BF16)).astype(BF16).reshape(8, 32, 256)

    pltpu.make_async_copy(lab2_in.at[pl.ds(0, 15)], lab2_in.at[pl.ds(0, 15)], lab_rs.at[1]).wait()
    lab = lab2_in[...].reshape(16, 128)
    lab = jnp.concatenate([lab, lab], axis=1)
    lane_label = jnp.sum(jnp.where(c16 // 16 == r16, lab, 0), axis=0, keepdims=True)
    hr, _ = rc(64, 256)
    picker = onehot(jnp.broadcast_to(lane_label, (64, 256)) == 2 * (hr % 32) + hr // 32 + 1)
    pltpu.make_async_copy(
        recv.at[pl.ds(0, N_DEV - 1)], recv.at[pl.ds(0, N_DEV - 1)], pay_rs
    ).wait()
    wide[...] = recv[...].reshape(2048, 128).astype(F32)
    fields = []
    for q in range(8):
        block = wide[pl.ds(q, 256, stride=8), :].astype(BF16)
        part = mm(picker, block)
        fields.append(jnp.concatenate([part[0:32], part[32:64]], axis=1).astype(BF16))
    for q in range(8):
        rem_ref[q] = fields[q]
    remap = mm(perm, jnp.concatenate(fields, axis=0))
    mis_ref[...] = ((fore[...] - remap) * (1.0 / 1024.0)).astype(BF16)

    def grad_pair(m, carry):
        head, acc = carry
        at = pl.multiple_of(m * 16, 16)
        to = pl.multiple_of(m * 128, 128)
        mis = mis_ref[pl.ds(at, 16), :]
        slope = (mm(bd_read, mis) * dsl[pl.ds(to, 128), :]).astype(BF16)
        head = head + nt(mis, hid[pl.ds(to, 128), :])
        window = jnp.concatenate([p3[j, pl.ds(at, 48), :] for j in range(3)], axis=0)
        return head, acc + nt(window, slope)

    head, acc = lax.fori_loop(
        0, 16, grad_pair,
        (jnp.zeros((16, 128), F32), jnp.zeros((144, 128), F32)),
        unroll=GRAD_UNROLL,
    )
    pairs = []
    for t in range(9):
        i, j = divmod(t, 3)
        at = 48 * j + 8 * i + 8
        pairs.append((acc[at : at + 8], acc[at + 8 : at + 16]))
    pairs.append((head[0:8], head[8:16]))
    low = lax.broadcasted_iota(I32, (8, 128), 1) < 64
    parts = []
    for b in range(5):
        a0, b0 = pairs[b]
        a1, b1 = pairs[b + 5]
        parts.append(
            jnp.where(low, a0 + pltpu.roll(b0, 64, 1), pltpu.roll(a1, 64, 1) + b1)
        )
    mine = jnp.concatenate(parts, axis=0)
    tbuf[...] = mine
    arr1[pl.ds(group, 1)] = mine[None]
    for k in (4, 5, 2, 3, 6, 7, 1):
        other = lax.rem(group + k, 8)
        pltpu.make_async_remote_copy(
            tbuf, arr1.at[group], ar_ss.at[0], ar1_rs,
            device_id=home + at_xc(other // 2, other % 2), device_id_type=LOGICAL,
        ).start()
    pltpu.make_async_copy(arr1.at[pl.ds(0, 7)], arr1.at[pl.ds(0, 7)], ar1_rs).wait()
    total = arr1[0]
    for k in range(1, 8):
        total = total + arr1[k]
    sum1[...] = total
    arr2[pl.ds(spot, 1)] = total[None]
    for dy, dz in ring:
        pltpu.make_async_remote_copy(
            sum1, arr2.at[spot], ar_ss.at[1], ar2_rs,
            device_id=in_ring(dy, dz)[1], device_id_type=LOGICAL,
        ).start()
    pltpu.make_async_copy(arr2.at[pl.ds(0, 15)], arr2.at[pl.ds(0, 15)], ar2_rs).wait()
    total = arr2[0]
    for k in range(1, 16):
        total = total + arr2[k]
    tot_ref[...] = total

    pltpu.make_async_copy(lab1_in.at[pl.ds(0, 7)], lab1_in.at[pl.ds(0, 7)], lab_ss.at[0]).wait()
    pltpu.make_async_copy(lab2_in.at[pl.ds(0, 15)], lab2_in.at[pl.ds(0, 15)], lab_ss.at[1]).wait()
    pltpu.make_async_copy(
        send.at[pl.ds(0, N_DEV - 1)], send.at[pl.ds(0, N_DEV - 1)], pay_ss
    ).wait()
    pltpu.make_async_copy(
        arr1.at[pl.ds(0, 7)], arr1.at[pl.ds(0, 7)], ar_ss.at[0]
    ).wait()
    pltpu.make_async_copy(
        arr2.at[pl.ds(0, 15)], arr2.at[pl.ds(0, 15)], ar_ss.at[1]
    ).wait()


def final_kernel(
    tot_any, rem_any, est_any, lift, kern, rem_out, est_out, gl_out, gk_out, gh_out, tot, sem
):
    moves = [
        pltpu.make_async_copy(tot_any, tot, sem.at[0]),
        pltpu.make_async_copy(rem_any, rem_out, sem.at[1]),
        pltpu.make_async_copy(est_any, est_out, sem.at[2]),
    ]
    for m in moves:
        m.start()
    moves[0].wait()

    def split(x):
        a = x.astype(BF16)
        x = x - a.astype(F32)
        b = x.astype(BF16)
        x = x - b.astype(F32)
        return a, b, x.astype(BF16)

    blocks = []
    for b in range(10):
        v = tot[(b % 5) * 8 : (b % 5) * 8 + 8, :]
        if b >= 5:
            v = pltpu.roll(v, 64, 1)
        if b == 9:
            gh_out[...] = v[:, 0:64]
            break
        parts = [p.astype(F32) for p in split(v)]
        parts.append(jnp.zeros((8, 128), F32))
        blocks.append(jnp.concatenate(parts, axis=0).astype(BF16)[:, 0:64])
    er, ec = rc(64, 64)
    eye = onehot(er == ec)
    liftf = lift[...].astype(F32)
    lift4 = jnp.concatenate([liftf] * 4, axis=0).astype(BF16)
    lift_t = nt(eye, lift4).astype(BF16)
    grad_lift = jnp.zeros((32, 64), F32)
    for t in range(9):
        gk_out[t] = mm(lift_t, blocks[t])
        grad_lift = grad_lift + nt(blocks[t], kern[t])
    gl_out[...] = grad_lift[0:8] + grad_lift[8:16] + grad_lift[16:24]
    moves[1].wait()
    moves[2].wait()


def per_device(source, weight, dest_tile, dest_row, prior, lift, kern, read):
    any_spec = pl.BlockSpec(memory_space=pl.ANY)
    hbm = pl.BlockSpec(memory_space=pltpu.HBM)
    vmem = pl.BlockSpec(memory_space=pltpu.VMEM)
    V = pltpu.VMEM
    DMA = pltpu.SemaphoreType.DMA
    rem, est, tot = pl.pallas_call(
        step_kernel,
        out_shape=(
            jax.ShapeDtypeStruct((8, 32, 256), BF16),
            jax.ShapeDtypeStruct((8, 32, 256), BF16),
            jax.ShapeDtypeStruct((40, 128), F32),
        ),
        in_specs=[hbm] * 8,
        out_specs=(vmem, vmem, vmem),
        scratch_shapes=[
            V((32, 8, 128), BF16), V((32, 4, 128, 128), BF16), V((4, 32), I32), V((4, 32), I32),
            V((8, 32, 256), BF16), V((8, 64), BF16), V((9, 64, 64), BF16), V((8, 64), BF16),
            V((128, 8, 128), F32), V((1, 256), I32), pltpu.SMEM((1, 256), I32),
            V((8, 1, 128), I32), V((8, 1, 128), I32), V((16, 1, 128), I32), V((16, 1, 128), I32),
            V((128, 16, 128), BF16), V((128, 16, 128), BF16), V((2048, 128), F32),
            V((16, 256), BF16), V((16, 256), BF16), V((6, 16, 256), BF16), V((2, 16, 256), BF16),
            V((3, 288, 256), BF16), V((36 * 192, 256), BF16), V((128, 768), BF16),
            V((256, 256), F32), V((256, 256), BF16), V((2048, 256), BF16), V((2048, 256), F32),
            V((2, 256, 128), BF16), V((8, 40, 128), F32), V((16, 40, 128), F32), V((40, 128), F32), V((40, 128), F32),
            DMA((7,)), DMA((WEIGHT_CHUNKS,)), DMA, DMA((2,)), DMA((2,)), DMA, DMA,
            DMA((8,)), DMA((8,)), DMA((2,)), DMA, DMA,
        ],
        compiler_params=pltpu.CompilerParams(
            collective_id=0, has_side_effects=True, vmem_limit_bytes=40 << 20
        ),
        name="step",
    )(*(
        pltpu.with_memory_space_constraint(x, pltpu.HBM)
        for x in (source, weight, dest_tile.T, dest_row.T, prior, lift, kern, read.T)
    ))
    rem, est, gl, gk, gh = pl.pallas_call(
        final_kernel,
        out_shape=(
            jax.ShapeDtypeStruct((8, 32, 256), BF16),
            jax.ShapeDtypeStruct((8, 32, 256), BF16),
            jax.ShapeDtypeStruct((8, 64), F32),
            jax.ShapeDtypeStruct((9, 64, 64), F32),
            jax.ShapeDtypeStruct((8, 64), F32),
        ),
        in_specs=[any_spec] * 3 + [vmem] * 2,
        out_specs=(hbm, hbm, vmem, vmem, vmem),
        scratch_shapes=[V((40, 128), F32), DMA((3,))],
        compiler_params=pltpu.CompilerParams(vmem_limit_bytes=16 << 20),
        name="final",
    )(tot, rem, est, lift, kern)
    return rem, est, gl, gk, gh.T


def solution(mesh):
    return jax.shard_map(
        per_device,
        mesh=mesh,
        in_specs=(
            P(("face", "lon"), None, None),
            P(("face", "lon"), None, None, None),
            P(("face", "lon"), None),
            P(("face", "lon"), None),
            P(None, "face", "lon"),
            P(),
            P(),
            P(),
        ),
        out_specs=(P(None, "face", "lon"), P(None, "face", "lon"), P(), P(), P()),
        check_vma=False,
    )
```

```python
import jax
import jax.numpy as jnp
from jax import lax
from jax.experimental import pallas as pl
from jax.experimental.pallas import tpu as pltpu
from jax.sharding import PartitionSpec as P

MESH, LOGICAL = pl.DeviceIdType.MESH, pl.DeviceIdType.LOGICAL
F32, BF16, I32 = jnp.float32, jnp.bfloat16, jnp.int32
N_FACE, N_LON = 8, 16
N_DEV = N_FACE * N_LON
NT = (((1,), (1,)), ((), ()))
WEIGHT_CHUNKS = 4
CONV_UNROLL, GRAD_UNROLL = 16, 16


def mm(a, b):
    return jnp.dot(a, b, preferred_element_type=F32)


def nt(a, b):
    return lax.dot_general(a, b, NT, preferred_element_type=F32)


def rc(rows, cols):
    return (
        lax.broadcasted_iota(I32, (rows, cols), 0),
        lax.broadcasted_iota(I32, (rows, cols), 1),
    )


def onehot(mask):
    return jnp.where(mask, 1.0, 0.0).astype(BF16)


FAR_FIRST = sorted(
    [
        (dy, dx, dz, dc)
        for dy in range(4) for dx in range(4) for dz in range(4) for dc in range(2)
    ][1:],
    key=lambda d: -sum(min(v, 4 - v) for v in d[:3]),
)


def step_kernel(
    src_hbm, wts_hbm, tile_hbm, row_hbm, prior_hbm, lift_hbm, kern_hbm, read_hbm,
    rem_ref, est_ref, tot_ref,
    src, wts, dtile, drow, prior, lift, kern, read,
    contrib, idx_v, idx_s, lab1_out, lab1_in, lab2_out, lab2_in, send, recv, wide,
    er_out, ec_out, er_in, ec_in, p3, l3, wconv, fore, mis_ref, hid, dsl, edges, arr1, arr2, sum1,
    tbuf,
    in_sem, w_sem, idx_sem, lab_ss, lab_rs, pay_ss, pay_rs,
    halo_ss, halo_rs, ar_ss, ar1_rs, ar2_rs,
):
    face = lax.axis_index("face")
    lon = lax.axis_index("lon")
    me = face * N_LON + lon
    y, z = face // 2, lon // 4
    x = (face % 2) * 2 + (lon // 2) % 2
    core = lon % 2
    group, spot = x * 2 + core, y * 4 + z
    home = y * 32 + z * 4
    here = spot * 8 + group

    def at_xc(x_at, core_at):
        return (x_at // 2) * 16 + (x_at % 2) * 2 + core_at

    barrier = pltpu.get_barrier_semaphore()

    y_at = [lax.rem(y + d, 4) * 32 for d in range(4)]
    x_at = [at_xc(lax.rem(x + d, 4), 0) for d in range(4)]
    zc_at = [lax.rem(z + d // 2, 4) * 4 + lax.rem(core + d % 2, 2) for d in range(8)]

    def others(action, order=FAR_FIRST):
        for dy, dx, dz, dc in order:
            action(y_at[dy] + x_at[dx] + zc_at[2 * dz + dc])

    def greet(other):
        pl.semaphore_signal(barrier, inc=1, device_id=other, device_id_type=LOGICAL)

    others(greet, FAR_FIRST[:40])
    small = [
        (tile_hbm, dtile), (row_hbm, drow), (prior_hbm, prior), (src_hbm, src),
        (lift_hbm, lift), (kern_hbm, kern), (read_hbm, read),
    ]
    loads = [pltpu.make_async_copy(a, b, in_sem.at[i]) for i, (a, b) in enumerate(small)]
    for c in loads:
        c.start()
    per = 32 // WEIGHT_CHUNKS
    wloads = [
        pltpu.make_async_copy(
            wts_hbm.at[pl.ds(i * per, per)], wts.at[pl.ds(i * per, per)], w_sem.at[i]
        )
        for i in range(WEIGHT_CHUNKS)
    ]
    for c in wloads:
        c.start()

    others(greet, FAR_FIRST[40:])
    for c in loads:
        c.wait()

    ri, ci = rc(128, 128)
    tiles, rows = dtile[...], drow[...]
    d_row = jnp.concatenate([tiles[k : k + 1] for k in range(4)], axis=1)
    l_row = jnp.concatenate([rows[k : k + 1] for k in range(4)], axis=1)
    d_mat = jnp.broadcast_to(d_row, (128, 128))
    d_col = d_mat.T
    rank = jnp.sum(jnp.where((d_col == d_mat) & (ri < ci), 1, 0), axis=0, keepdims=True)
    pos = jnp.broadcast_to(2 * d_row + rank, (128, 128)).T
    idx_v[...] = jnp.concatenate(
        [
            jnp.sum(jnp.where(pos == ci + at, ri, 0), axis=0, keepdims=True)
            for at in (0, 128)
        ],
        axis=1,
    )
    idx_copy = pltpu.make_async_copy(idx_v, idx_s, idx_sem)
    idx_copy.start()
    l_col = jnp.broadcast_to(l_row, (128, 128)).T
    spots = (d_col // 32) * 4 + (d_col // 4) % 4
    labels = jnp.where(spots * 2 + pos - 2 * d_col == ci, l_col + 1, 0).astype(F32).astype(BF16)
    d_few = d_mat[0:16]
    owners = onehot(((d_few // 16) % 2) * 4 + d_few % 4 == ri[0:16])
    lab1_out[...] = mm(owners, labels)[0:8].astype(I32).reshape(8, 1, 128)
    lab1_in[pl.ds(group, 1)] = lab1_out[pl.ds(group, 1)]

    r, c = rc(256, 256)
    perm = onehot((r // 8 == c % 32) & (r % 8 == c // 32))
    shift0 = onehot(r == c - 1)
    shift2 = onehot(r == c + 1)
    eye = onehot(r == c)
    pf = mm(perm, prior[...].reshape(256, 256))
    pb = pf.astype(BF16)
    p3[1, pl.ds(16, 256), :] = pb
    er_out[...] = jnp.concatenate([pf[0:8], pf[248:256]], axis=0).astype(BF16)
    r16, c16 = rc(16, 256)
    edge = onehot(((r16 == 0) & (c16 == 0)) | ((r16 == 1) & (c16 == 255)))
    ec_out[...] = nt(edge, pb).astype(BF16)

    for chunk in range(WEIGHT_CHUNKS):
        wloads[chunk].wait()

        def regrid(s, carry):
            block = jnp.concatenate([wts[s, k] for k in range(4)], axis=1)
            out = mm(src[s], block)
            for k in range(4):
                contrib[k * 32 + s] = out[:, k * 128 : (k + 1) * 128].astype(BF16).astype(F32)
            return carry

        lax.fori_loop(chunk * per, (chunk + 1) * per, regrid, 0, unroll=per)
    idx_copy.wait()

    def place(d, carry):
        a = contrib[idx_s[0, 2 * d]]
        b = contrib[idx_s[0, 2 * d + 1]]
        send[d] = jnp.concatenate([a, b], axis=0).astype(BF16)
        return carry

    lax.fori_loop(0, N_DEV, place, 0, unroll=16)
    recv[pl.ds(here, 1)] = send[pl.ds(me, 1)]

    pl.semaphore_wait(barrier, N_DEV - 1)

    up, down = lax.rem(face + N_FACE - 1, N_FACE), lax.rem(face + 1, N_FACE)
    left, right = lax.rem(lon + N_LON - 1, N_LON), lax.rem(lon + 1, N_LON)
    halos = []
    ways = [(up, left), (up, lon), (up, right), (down, left), (down, lon), (down, right)]
    for k, (f, l) in enumerate(ways):
        halos.append(
            pltpu.make_async_remote_copy(
                er_out, er_in.at[5 - k], halo_ss.at[k], halo_rs.at[5 - k],
                device_id=(f, l), device_id_type=MESH,
            )
        )
    for k, l in enumerate((left, right)):
        halos.append(
            pltpu.make_async_remote_copy(
                ec_out, ec_in.at[1 - k], halo_ss.at[6 + k], halo_rs.at[7 - k],
                device_id=(face, l), device_id_type=MESH,
            )
        )
    for h in halos:
        h.start()
    for k in (4, 5, 2, 3, 6, 7, 1):
        other = lax.rem(group + k, 8)
        pltpu.make_async_remote_copy(
            lab1_out.at[other], lab1_in.at[group], lab_ss.at[0], lab_rs.at[0],
            device_id=home + at_xc(other // 2, other % 2), device_id_type=LOGICAL,
        ).start()

    i64r, i64c = rc(128, 64)
    eye2 = onehot(i64r % 64 == i64c)
    liftf = lift[...].astype(F32)
    lift2 = jnp.concatenate([liftf, liftf], axis=0).astype(BF16)
    br, bc = rc(128, 16)
    block_mask = br // 64 == bc // 8
    bd_lift = jnp.where(block_mask, nt(eye2, lift2), 0.0).astype(BF16)
    readf = read[...].astype(F32)
    read2 = jnp.concatenate([readf, readf], axis=0).astype(BF16)
    bd_read = jnp.where(block_mask, nt(eye2, read2), 0.0).astype(BF16)
    tr, tc = rc(16, 128)
    bd_read_t = jnp.where(
        tr // 8 == tc // 64,
        jnp.concatenate([jnp.concatenate([readf, readf], axis=1)] * 2, axis=0),
        0.0,
    ).astype(BF16)
    taps = kern[...].reshape(576, 64)
    zeros = jnp.zeros((192, 64), BF16)
    eye1 = eye2[0:64]
    wconv[0:64, :] = nt(eye1, jnp.concatenate([taps, zeros], axis=0)).astype(BF16)
    wconv[64:128, :] = nt(eye1, jnp.concatenate([zeros, taps], axis=0)).astype(BF16)

    p3[0, pl.ds(16, 256), :] = mm(pb, shift0).astype(BF16)
    p3[2, pl.ds(16, 256), :] = mm(pb, shift2).astype(BF16)

    def lift_pair(m, carry):
        at = pl.multiple_of(m * 16, 16)
        for j in range(3):
            out = mm(bd_lift, p3[j, pl.ds(at, 16), :]).astype(BF16)
            for e in range(2):
                to = pl.multiple_of((2 * m + e) * 192 + j * 64, 64)
                l3[pl.ds(to, 64), :] = out[e * 64 : (e + 1) * 64]
        return carry

    def send_block(other):
        pltpu.make_async_remote_copy(
            send.at[other], recv.at[here], pay_ss, pay_rs,
            device_id=other, device_id_type=LOGICAL,
        ).start()

    others(send_block)
    for m in range(1, 17):
        lift_pair(m, 0)

    pltpu.make_async_copy(lab1_in.at[pl.ds(0, 7)], lab1_in.at[pl.ds(0, 7)], lab_rs.at[0]).wait()
    came = lab1_in[...].reshape(8, 128).astype(F32).astype(BF16)
    vr, vc = rc(128, 8)
    spread = mm(onehot((vr % 16) // 2 == vc), came)
    spread = jnp.where(ri % 2 == ci % 2, spread, 0.0).astype(BF16)
    lab2_out[...] = (
        nt(onehot(ri[0:16] == ci[0:16] // 2), spread).astype(I32).reshape(16, 1, 128)
    )
    lab2_in[pl.ds(spot, 1)] = lab2_out[pl.ds(spot, 1)]
    place_xc = at_xc(x, core)
    ring = sorted(
        ((dy, dz) for dy in range(4) for dz in range(4)),
        key=lambda d: -(min(d[0], 4 - d[0]) + min(d[1], 4 - d[1])),
    )[:-1]

    def in_ring(dy, dz):
        there_y, there_z = lax.rem(y + dy, 4), lax.rem(z + dz, 4)
        return there_y * 4 + there_z, there_y * 32 + there_z * 4 + place_xc

    for dy, dz in ring:
        other, device = in_ring(dy, dz)
        pltpu.make_async_remote_copy(
            lab2_out.at[other], lab2_in.at[spot], lab_ss.at[1], lab_rs.at[1],
            device_id=device, device_id_type=LOGICAL,
        ).start()

    for h in halos:
        h.wait()
    keep_up = jnp.where(face > 0, 1.0, 0.0)
    keep_down = jnp.where(face < N_FACE - 1, 1.0, 0.0)
    z8 = jnp.zeros((8, 256), F32)

    def rows_of(k):
        upper = er_in[k].astype(F32)[8:16] * keep_up
        lower = er_in[k + 3].astype(F32)[0:8] * keep_down
        return jnp.concatenate([z8, upper, lower, z8], axis=0).astype(BF16)

    corner0 = onehot((r == 255) & (c == 0))
    corner2 = onehot((r == 0) & (c == 255))
    mid, lef, rig = rows_of(1), rows_of(0), rows_of(2)
    outer0 = (mm(mid, shift0) + mm(lef, corner0)).astype(BF16)
    outer2 = (mm(mid, shift2) + mm(rig, corner2)).astype(BF16)
    for j, outer in ((0, outer0), (1, mid), (2, outer2)):
        p3[j, pl.ds(0, 16), :] = outer[0:16]
        p3[j, pl.ds(272, 16), :] = outer[16:32]
    for e, lane in ((0, 0), (1, 127)):
        sel = onehot((c16[:, 0:128] == lane) & (r16[:, 0:128] == 1 - e))
        column = mm(nt(eye, ec_in[e]).astype(BF16), sel).astype(BF16)
        at = pl.ds(128 * e, 128)
        p3[2 * e, pl.ds(16, 256), at] = p3[2 * e, pl.ds(16, 256), at] + column
        edges[e] = column
    edges[0] = edges[0] + edges[1]

    for m in (0, 17):
        lift_pair(m, 0)

    low_lanes = ci < 64
    for m in range(16):
        both = mm(bd_lift, edges[0, 16 * m : 16 * m + 16, :])
        for e, keep in ((0, low_lanes), (1, jnp.logical_not(low_lanes))):
            column = jnp.where(keep, both, 0.0).astype(BF16)
            at = pl.ds(128 * e, 128)
            for k in range(2):
                to = pl.ds((2 * m + 2 + k) * 192 + 128 * e, 64)
                l3[to, at] = l3[to, at] + column[k * 64 : (k + 1) * 64]

    def conv_of(m):
        at = pl.multiple_of((2 * m + 1) * 192, 64)
        return mm(wconv[...], l3[pl.ds(at, 768), :])

    def activate(m, act):
        to = pl.multiple_of(m * 128, 128)
        sig = 0.5 * jnp.tanh(0.5 * act) + 0.5
        value = act * sig
        hid[pl.ds(to, 128), :] = value.astype(BF16)
        dsl[pl.ds(to, 128), :] = sig + value * (1.0 - sig)

    def conv_pair(m, carry):
        activate(m, conv_of(m))
        return carry

    lax.fori_loop(0, 16, conv_pair, 0, unroll=CONV_UNROLL)

    def read_pair(m, carry):
        to = pl.multiple_of(m * 128, 128)
        row = pl.multiple_of(m * 16, 16)
        prow = pl.multiple_of(m * 16 + 16, 16)
        fore[pl.ds(row, 16), :] = p3[1, pl.ds(prow, 16), :].astype(F32) + mm(
            bd_read_t, hid[pl.ds(to, 128), :]
        )
        return carry

    lax.fori_loop(0, 16, read_pair, 0, unroll=4)
    perm_t = onehot((r // 32 == c % 8) & (r % 32 == c // 8))
    est_ref[...] = mm(perm_t, fore[...].astype(BF16)).astype(BF16).reshape(8, 32, 256)

    pltpu.make_async_copy(lab2_in.at[pl.ds(0, 15)], lab2_in.at[pl.ds(0, 15)], lab_rs.at[1]).wait()
    lab = lab2_in[...].reshape(16, 128)
    lab = jnp.concatenate([lab, lab], axis=1)
    lane_label = jnp.sum(jnp.where(c16 // 16 == r16, lab, 0), axis=0, keepdims=True)
    hr, _ = rc(64, 256)
    picker = onehot(jnp.broadcast_to(lane_label, (64, 256)) == 2 * (hr % 32) + hr // 32 + 1)
    pltpu.make_async_copy(
        recv.at[pl.ds(0, N_DEV - 1)], recv.at[pl.ds(0, N_DEV - 1)], pay_rs
    ).wait()
    wide[pl.ds(0, 2048), :] = recv[...].reshape(2048, 128).astype(F32)
    fields = []
    for q in range(8):
        block = wide[pl.ds(q, 256, stride=8), :].astype(BF16)
        part = mm(picker, block)
        fields.append(jnp.concatenate([part[0:32], part[32:64]], axis=1).astype(BF16))
    for q in range(8):
        rem_ref[q] = fields[q]
    remap = mm(perm, jnp.concatenate(fields, axis=0))
    mis_ref[...] = ((fore[...] - remap) * (1.0 / 1024.0)).astype(BF16)

    def grad_pair(m, carry):
        head, acc = carry
        at = pl.multiple_of(m * 16, 16)
        to = pl.multiple_of(m * 128, 128)
        mis = mis_ref[pl.ds(at, 16), :]
        slope = (mm(bd_read, mis) * dsl[pl.ds(to, 128), :]).astype(BF16)
        head = head + nt(mis, hid[pl.ds(to, 128), :])
        window = jnp.concatenate([p3[j, pl.ds(at, 48), :] for j in range(3)], axis=0)
        return head, acc + nt(window, slope)

    head, acc = lax.fori_loop(
        0, 16, grad_pair,
        (jnp.zeros((16, 128), F32), jnp.zeros((144, 128), F32)),
        unroll=GRAD_UNROLL,
    )
    pairs = []
    for t in range(9):
        i, j = divmod(t, 3)
        at = 48 * j + 8 * i + 8
        pairs.append((acc[at : at + 8], acc[at + 8 : at + 16]))
    pairs.append((head[0:8], head[8:16]))
    low = lax.broadcasted_iota(I32, (8, 128), 1) < 64
    parts = []
    for b in range(5):
        a0, b0 = pairs[b]
        a1, b1 = pairs[b + 5]
        parts.append(
            jnp.where(low, a0 + pltpu.roll(b0, 64, 1), pltpu.roll(a1, 64, 1) + b1)
        )
    mine = jnp.concatenate(parts, axis=0)
    tbuf[...] = mine
    arr1[pl.ds(group, 1)] = mine[None]
    for k in (4, 5, 2, 3, 6, 7, 1):
        other = lax.rem(group + k, 8)
        pltpu.make_async_remote_copy(
            tbuf, arr1.at[group], ar_ss.at[0], ar1_rs,
            device_id=home + at_xc(other // 2, other % 2), device_id_type=LOGICAL,
        ).start()
    pltpu.make_async_copy(arr1.at[pl.ds(0, 7)], arr1.at[pl.ds(0, 7)], ar1_rs).wait()
    total = arr1[0]
    for k in range(1, 8):
        total = total + arr1[k]
    sum1[...] = total
    arr2[pl.ds(spot, 1)] = total[None]
    for dy, dz in ring:
        pltpu.make_async_remote_copy(
            sum1, arr2.at[spot], ar_ss.at[1], ar2_rs,
            device_id=in_ring(dy, dz)[1], device_id_type=LOGICAL,
        ).start()
    pltpu.make_async_copy(arr2.at[pl.ds(0, 15)], arr2.at[pl.ds(0, 15)], ar2_rs).wait()
    total = arr2[0]
    for k in range(1, 16):
        total = total + arr2[k]
    tot_ref[...] = total

    pltpu.make_async_copy(lab1_in.at[pl.ds(0, 7)], lab1_in.at[pl.ds(0, 7)], lab_ss.at[0]).wait()
    pltpu.make_async_copy(lab2_in.at[pl.ds(0, 15)], lab2_in.at[pl.ds(0, 15)], lab_ss.at[1]).wait()
    pltpu.make_async_copy(
        send.at[pl.ds(0, N_DEV - 1)], send.at[pl.ds(0, N_DEV - 1)], pay_ss
    ).wait()
    pltpu.make_async_copy(
        arr1.at[pl.ds(0, 7)], arr1.at[pl.ds(0, 7)], ar_ss.at[0]
    ).wait()
    pltpu.make_async_copy(
        arr2.at[pl.ds(0, 15)], arr2.at[pl.ds(0, 15)], ar_ss.at[1]
    ).wait()


def final_kernel(
    tot_any, rem_any, est_any, lift, kern, rem_out, est_out, gl_out, gk_out, gh_out, tot, sem
):
    moves = [
        pltpu.make_async_copy(tot_any, tot, sem.at[0]),
        pltpu.make_async_copy(rem_any, rem_out, sem.at[1]),
        pltpu.make_async_copy(est_any, est_out, sem.at[2]),
    ]
    for m in moves:
        m.start()
    moves[0].wait()

    def split(x):
        a = x.astype(BF16)
        x = x - a.astype(F32)
        b = x.astype(BF16)
        x = x - b.astype(F32)
        return a, b, x.astype(BF16)

    blocks = []
    for b in range(10):
        v = tot[(b % 5) * 8 : (b % 5) * 8 + 8, :]
        if b >= 5:
            v = pltpu.roll(v, 64, 1)
        if b == 9:
            gh_out[...] = v[:, 0:64]
            break
        parts = [p.astype(F32) for p in split(v)]
        parts.append(jnp.zeros((8, 128), F32))
        blocks.append(jnp.concatenate(parts, axis=0).astype(BF16)[:, 0:64])
    er, ec = rc(64, 64)
    eye = onehot(er == ec)
    liftf = lift[...].astype(F32)
    lift4 = jnp.concatenate([liftf] * 4, axis=0).astype(BF16)
    lift_t = nt(eye, lift4).astype(BF16)
    grad_lift = jnp.zeros((32, 64), F32)
    for t in range(9):
        gk_out[t] = mm(lift_t, blocks[t])
        grad_lift = grad_lift + nt(blocks[t], kern[t])
    gl_out[...] = grad_lift[0:8] + grad_lift[8:16] + grad_lift[16:24]
    moves[1].wait()
    moves[2].wait()


def per_device(source, weight, dest_tile, dest_row, prior, lift, kern, read):
    any_spec = pl.BlockSpec(memory_space=pl.ANY)
    hbm = pl.BlockSpec(memory_space=pltpu.HBM)
    vmem = pl.BlockSpec(memory_space=pltpu.VMEM)
    V = pltpu.VMEM
    DMA = pltpu.SemaphoreType.DMA
    rem, est, tot = pl.pallas_call(
        step_kernel,
        out_shape=(
            jax.ShapeDtypeStruct((8, 32, 256), BF16),
            jax.ShapeDtypeStruct((8, 32, 256), BF16),
            jax.ShapeDtypeStruct((40, 128), F32),
        ),
        in_specs=[hbm] * 8,
        out_specs=(vmem, vmem, vmem),
        scratch_shapes=[
            V((32, 8, 128), BF16), V((32, 4, 128, 128), BF16), V((4, 32), I32), V((4, 32), I32),
            V((8, 32, 256), BF16), V((8, 64), BF16), V((9, 64, 64), BF16), V((8, 64), BF16),
            V((128, 8, 128), F32), V((1, 256), I32), pltpu.SMEM((1, 256), I32),
            V((8, 1, 128), I32), V((8, 1, 128), I32), V((16, 1, 128), I32), V((16, 1, 128), I32),
            V((128, 16, 128), BF16), V((128, 16, 128), BF16), V((2056, 128), F32),
            V((16, 256), BF16), V((16, 256), BF16), V((6, 16, 256), BF16), V((2, 16, 256), BF16),
            V((3, 288, 256), BF16), V((36 * 192, 256), BF16), V((128, 768), BF16),
            V((256, 256), F32), V((256, 256), BF16), V((2048, 256), BF16), V((2048, 256), F32),
            V((2, 256, 128), BF16), V((8, 40, 128), F32), V((16, 40, 128), F32), V((40, 128), F32), V((40, 128), F32),
            DMA((7,)), DMA((WEIGHT_CHUNKS,)), DMA, DMA((2,)), DMA((2,)), DMA, DMA,
            DMA((8,)), DMA((8,)), DMA((2,)), DMA, DMA,
        ],
        compiler_params=pltpu.CompilerParams(
            collective_id=0, has_side_effects=True, vmem_limit_bytes=40 << 20
        ),
        name="step",
    )(*(
        pltpu.with_memory_space_constraint(x, pltpu.HBM)
        for x in (source, weight, dest_tile.T, dest_row.T, prior, lift, kern, read.T)
    ))
    rem, est, gl, gk, gh = pl.pallas_call(
        final_kernel,
        out_shape=(
            jax.ShapeDtypeStruct((8, 32, 256), BF16),
            jax.ShapeDtypeStruct((8, 32, 256), BF16),
            jax.ShapeDtypeStruct((8, 64), F32),
            jax.ShapeDtypeStruct((9, 64, 64), F32),
            jax.ShapeDtypeStruct((8, 64), F32),
        ),
        in_specs=[any_spec] * 3 + [vmem] * 2,
        out_specs=(hbm, hbm, vmem, vmem, vmem),
        scratch_shapes=[V((40, 128), F32), DMA((3,))],
        compiler_params=pltpu.CompilerParams(vmem_limit_bytes=16 << 20),
        name="final",
    )(tot, rem, est, lift, kern)
    return rem, est, gl, gk, gh.T


def solution(mesh):
    return jax.shard_map(
        per_device,
        mesh=mesh,
        in_specs=(
            P(("face", "lon"), None, None),
            P(("face", "lon"), None, None, None),
            P(("face", "lon"), None),
            P(("face", "lon"), None),
            P(None, "face", "lon"),
            P(),
            P(),
            P(),
        ),
        out_specs=(P(None, "face", "lon"), P(None, "face", "lon"), P(), P(), P()),
        check_vma=False,
    )
```
